32 devices in a mesh: dp: 8 (over y, x, core), mp: 4 (over z).
Axes of the slice: x: 2, y: 2, z: 4, core: 2. Of those that a mesh axis runs over, the one named last changes fastest.
Arguments:
- inputs: bfloat16 [8, 3072, 768], P('dp'), may hold values from -6 to 6
- counts: int32 [8], P('dp'), may hold values from 1024 to 3072, as said below
- first_gain: float32 [768], replicated, may hold values from 0.5 to 1.5
- first_bias: float32 [768], replicated, may hold values from -4 to 4
- query_key_value_weight: bfloat16 [768, 3, 768], P(None, None, 'mp'), may hold values from -0.21875 to 0.21875
- query_bias: float32 [768], P('mp'), may hold values from -6 to 6
- value_bias: float32 [768], P('mp'), may hold values from -0.75 to 0.75
- w_out: bfloat16 [768, 768], P('mp'), may hold values from -4 to 4
- out_bias: float32 [768], replicated, may hold values from -4 to 4
- second_gain: float32 [768], replicated, may hold values from 0.5 to 1.5
- second_bias: float32 [768], replicated, may hold values from -4 to 4
- w_up: bfloat16 [768, 3072], P(None, 'mp'), may hold values from -0.21875 to 0.21875
- up_bias: float32 [3072], P('mp'), may hold values from -4 to 4
- w_down: bfloat16 [3072, 768], P('mp'), may hold values from -0.109375 to 0.109375
- down_bias: float32 [768], replicated, may hold values from -4 to 4
- out_grad: bfloat16 [8, 3072, 768], P('dp'), may hold values from -6 to 6
Outputs:
- outputs: bfloat16 [8, 3072, 768], P('dp')
- input_grad: float32 [8, 3072, 768], P('dp')
- grad_first_gain: float32 [768], replicated
- grad_first_bias: float32 [768], replicated
- query_key_value_gradient: float32 [768, 3, 768], P(None, None, 'mp')
- grad_query_bias: float32 [768], P('mp')
- grad_value_bias: float32 [768], P('mp')
- grad_out: float32 [768, 768], P('mp')
- grad_out_bias: float32 [768], replicated
- grad_second_gain: float32 [768], replicated
- grad_second_bias: float32 [768], replicated
- grad_up: float32 [768, 3072], P(None, 'mp')
- grad_up_bias: float32 [3072], P('mp')
- grad_down: float32 [3072, 768], P('mp')
- grad_down_bias: float32 [768], replicated
The draws below stay inside these ranges and needn't reach their ends.
Inputs may be any that keep to these rules, and one draw needn't show every extreme that they name: `counts`: each cell's count lies between 1024 and 3072; the first cell has exactly 3072 genes.
All inputs are finite; a program needn't handle non-finite values.
Results may differ from the reference program's by a relative error of at most 0.012.
The reference program's roundings to bfloat16 on the way count: a program that leaves them out, or rounds other values in their place, can miss the bound.
Values may be sent and summed in bfloat16 or wider, within the bound.
A program may use at most 192 MiB of HBM per device.

```python
import jax
import jax.numpy as jnp
from jax import lax

D = 768
HEADS = 12
HEAD_DIM = 64
FF = 3072
PAD = 3072
QB = 512
CELLS = 8


def draw_counts(key, part):
    drawn = jax.random.randint(key, (CELLS,), PAD // 3, PAD + 1, dtype=jnp.int32)
    return drawn.at[0].set(PAD)


def block_levels(key, extent, pieces, least, top_value):
    factor_of = 1.0
    for dim, blocks in pieces:
        draws = jax.random.uniform(jax.random.fold_in(jax.random.fold_in(key, 6), dim), (blocks,), jnp.float32, least / len(pieces), top_value / len(pieces))
        factor_of = factor_of * jnp.repeat(jnp.exp(draws), extent[dim] // blocks).reshape((-1,) + (1,) * (len(extent) - 1 - dim))
    return factor_of


def gaussian(own_key, extent, deviation, reach, pieces=(), kind=jnp.bfloat16):
    values = jax.random.normal(own_key, extent, jnp.float32) * deviation
    if len(pieces) > 0:
        values = block_levels(own_key, extent, pieces, -0.22, 0.18) * values
    return jnp.clip(values, min=-reach, max=reach).astype(kind)


def setup_inputs(seed: int = 0) -> dict:
    key_of = jax.random.split(jax.random.key(seed), 17)
    inputs = gaussian(key_of[0], (CELLS, PAD, D), 1.0, 6.0, ((0, 8),))
    counts = draw_counts(jax.random.fold_in(key_of[16], 71), 0)
    first_gain = jnp.clip(1.0 + 0.1 * jax.random.normal(key_of[2], (D,), jnp.float32), 0.5, 1.5)
    first_bias = gaussian(key_of[3], (D,), 0.3, 4.0, (), jnp.float32)
    query_key_value_weight = gaussian(key_of[4], (D, 3, HEADS * HEAD_DIM), D ** -0.5, 0.21875, ((2, 4),))
    query_bias = gaussian(key_of[5], (HEADS * HEAD_DIM,), 0.5, 6.0, ((0, 4),), jnp.float32)
    value_bias = gaussian(key_of[6], (HEADS * HEAD_DIM,), 0.05, 0.75, ((0, 4),), jnp.float32)
    w_out = gaussian(key_of[7], (HEADS * HEAD_DIM, D), 2 ** -0.5, 4.0, ((0, 4),))
    out_bias = gaussian(key_of[8], (D,), 0.3, 4.0, (), jnp.float32)
    second_gain = jnp.clip(1.0 + 0.1 * jax.random.normal(key_of[9], (D,), jnp.float32), 0.5, 1.5)
    second_bias = gaussian(key_of[10], (D,), 0.3, 4.0, (), jnp.float32)
    w_up = gaussian(key_of[11], (D, FF), D ** -0.5, 0.21875, ((1, 4),))
    up_bias = gaussian(key_of[12], (FF,), 0.3, 4.0, ((0, 4),), jnp.float32)
    w_down = gaussian(key_of[13], (FF, D), FF ** -0.5, 0.109375, ((0, 4),))
    down_bias = gaussian(key_of[14], (D,), 0.3, 4.0, (), jnp.float32)
    out_grad = gaussian(key_of[15], (CELLS, PAD, D), 1.0, 6.0, ((0, 8),))
    return {"inputs": inputs, "counts": counts, "first_gain": first_gain, "first_bias": first_bias, "query_key_value_weight": query_key_value_weight, "query_bias": query_bias, "value_bias": value_bias, "w_out": w_out, "out_bias": out_bias, "second_gain": second_gain, "second_bias": second_bias, "w_up": w_up, "up_bias": up_bias, "w_down": w_down, "down_bias": down_bias, "out_grad": out_grad}


@jax.custom_vjp
def low(v):
    return lax.optimization_barrier(v.astype(jnp.bfloat16)).astype(jnp.float32)

@jax.custom_vjp
def low_back(v):
    return v

def low_keep(v):
    return (low(v), None)

def low_pass(kept, grad):
    return (grad,)

def back_keep(v):
    return (v, None)

def back_low(kept, grad):
    return (low(grad),)
low.defvjp(low_keep, low_pass)
low_back.defvjp(back_keep, back_low)

def layer_norm(row_block, scales, offset):
    centred = row_block - lax.optimization_barrier(jnp.mean(row_block, axis=-1, keepdims=True))
    variance = lax.optimization_barrier(jnp.mean(centred * centred, axis=-1, keepdims=True))
    return centred * lax.rsqrt(variance + 1e-05) * scales + offset

def cell_forward(params, row_in, length):
    first_gain, first_bias, query_key_value_weight, query_bias, value_bias, w_out, out_bias, second_gain, second_bias, w_up, up_bias, w_down, down_bias = params
    highest_precision = lax.Precision.HIGHEST
    keymask = jnp.arange(PAD) < length
    first_norm_input = low(layer_norm(row_in, first_gain, first_bias))
    projected_rows = jnp.einsum('yc,cur->uyr', first_norm_input, query_key_value_weight, precision=highest_precision)
    queries = low(low_back(projected_rows[0] + query_bias)).reshape(PAD, HEADS, HEAD_DIM)
    key_rows = low(low_back(projected_rows[1])).reshape(PAD, HEADS, HEAD_DIM)
    value_rows = low(low_back(projected_rows[2] + value_bias)).reshape(PAD, HEADS, HEAD_DIM)
    score_scale = HEAD_DIM ** (-0.5)

    def one_block(query_block):
        scores = jnp.einsum('qhd,khd->hqk', query_block, key_rows, precision=highest_precision) * score_scale
        scores = low_back(jnp.where(keymask[None, None, :], scores, -1e+30))
        maxima = lax.optimization_barrier(jnp.max(scores, axis=-1, keepdims=True))
        powers = jnp.exp(scores - maxima)
        weights = low(powers / lax.optimization_barrier(jnp.sum(powers, axis=-1, keepdims=True)))
        return jnp.einsum('hqk,khd->qhd', weights, value_rows, precision=highest_precision)
    context = lax.map(jax.checkpoint(one_block), queries.reshape(PAD // QB, QB, HEADS, HEAD_DIM))
    context = low(low_back(context.reshape(PAD, HEADS * HEAD_DIM)))
    mixed = row_in + low_back(jnp.dot(context, w_out, precision=highest_precision) + out_bias)
    second_in = low(layer_norm(mixed, second_gain, second_bias))
    up_input = low_back(jnp.dot(second_in, w_up, precision=highest_precision) + up_bias)
    activated = low(jax.nn.gelu(up_input, approximate=False))
    return mixed + low_back(jnp.dot(activated, w_down, precision=highest_precision) + down_bias)

def reference(inputs, counts, first_gain, first_bias, query_key_value_weight, query_bias, value_bias, w_out, out_bias, second_gain, second_bias, w_up, up_bias, w_down, down_bias, out_grad):
    params = (first_gain.astype(jnp.float32), first_bias.astype(jnp.float32), query_key_value_weight.astype(jnp.float32), query_bias.astype(jnp.float32), value_bias.astype(jnp.float32), w_out.astype(jnp.float32), out_bias.astype(jnp.float32), second_gain.astype(jnp.float32), second_bias.astype(jnp.float32), w_up.astype(jnp.float32), up_bias.astype(jnp.float32), w_down.astype(jnp.float32), down_bias.astype(jnp.float32))

    def forward(params, rows_in):

        def cell_step(carry, items):
            return (carry, cell_forward(params, items[0], items[1]))
        unused, result = lax.scan(cell_step, jnp.zeros((), jnp.float32), (rows_in, counts))
        return result
    outputs, pullback = jax.vjp(forward, params, inputs.astype(jnp.float32))
    valid = (jnp.arange(PAD)[None, :] < counts[:, None]).astype(jnp.float32)
    grads, input_grad = pullback(out_grad.astype(jnp.float32) * valid[:, :, None])
    return (outputs.astype(jnp.bfloat16), input_grad, grads[0], grads[1], grads[2], grads[3], grads[4], grads[5], grads[6], grads[7], grads[8], grads[9], grads[10], grads[11], grads[12])
```

```python
import functools

import jax
import jax.numpy as jnp
from jax import lax
from jax.experimental import pallas as pl
from jax.experimental.pallas import tpu as pltpu
from jax.sharding import PartitionSpec as P

HEAD_DIM = 64
LOG2E = 1.4426950408889634
EPS = 1e-05
BF = jnp.bfloat16
F32 = jnp.float32
NN = (((1,), (0,)), ((), ()))
NT = (((1,), (1,)), ((), ()))
TN = (((0,), (0,)), ((), ()))
VMEM_LIMIT = 62 * 2**20
MESH = pl.DeviceIdType.MESH


def mm(a, b, dims):
    return lax.dot_general(a, b, dims, preferred_element_type=F32)


def split3(v):
    a = v.astype(BF)
    rest = v - a.astype(F32)
    b = rest.astype(BF)
    return (a, b, (rest - b.astype(F32)).astype(BF))


def normed(rows):
    centred = rows - jnp.mean(rows, axis=-1, keepdims=True)
    inverse = lax.rsqrt(jnp.mean(centred * centred, axis=-1, keepdims=True) + EPS)
    return (centred * inverse, inverse)


def norm_back(grad, n, inverse, gain):
    t = grad * gain
    return inverse * (
        t - jnp.mean(t, axis=-1, keepdims=True) - n * jnp.mean(t * n, axis=-1, keepdims=True)
    )


def row_terms(v, count, width):
    a, b, c = split3(v)
    index = lax.broadcasted_iota(jnp.int32, (count, width), 0)
    spread = lambda t: jnp.broadcast_to(t.astype(F32), (count, width))
    zero = jnp.zeros((count, width), F32)
    picked = jnp.where(index == 2, spread(c), zero)
    picked = jnp.where(index == 1, spread(b), picked)
    return jnp.where(index == 0, spread(a), picked).astype(BF)


def front_kernel(in_ref, w_ref, bias_ref, gain_ref, first_ref, q_ref, k_ref, v_ref, *, width):
    n, _ = normed(in_ref[...].astype(F32))
    first = (n * gain_ref[0:1] + gain_ref[1:2]).astype(BF)
    first_ref[...] = first
    projected = mm(w_ref[...], first, NT) + bias_ref[...]
    q_ref[...] = projected[:width].astype(BF)
    k_ref[...] = projected[width : 2 * width].astype(BF)
    v_ref[...] = projected[2 * width :].astype(BF)


def front(rows, weight, bias, gains, block=512):
    count, features = rows.shape
    width = weight.shape[0] // 3
    row_spec = pl.BlockSpec((block, features), lambda i: (i, 0))
    out_spec = pl.BlockSpec((width, block), lambda i: (0, i))
    return pl.pallas_call(
        functools.partial(front_kernel, width=width),
        grid=(count // block,),
        in_specs=[
            row_spec,
            pl.BlockSpec(weight.shape, lambda i: (0, 0)),
            pl.BlockSpec(bias.shape, lambda i: (0, 0)),
            pl.BlockSpec(gains.shape, lambda i: (0, 0)),
        ],
        out_specs=[row_spec, out_spec, out_spec, out_spec],
        out_shape=[jax.ShapeDtypeStruct((count, features), BF)]
        + [jax.ShapeDtypeStruct((width, count), BF)] * 3,
        compiler_params=pltpu.CompilerParams(vmem_limit_bytes=VMEM_LIMIT),
        name="front",
    )(rows, weight, bias, gains)


def scaled_query(q):
    scaled = q.astype(F32) * (LOG2E * HEAD_DIM**-0.5)
    high = scaled.astype(BF)
    return (high, (scaled - high.astype(F32)).astype(BF))


def extended_keys(k, mask, with_ones):
    count = k.shape[1]
    index = lax.broadcasted_iota(jnp.int32, (128, count), 0)
    rest = 1.0 if with_ones else 0.0
    extra = jnp.where(
        index == 0,
        jnp.broadcast_to(mask, (128, count)),
        jnp.where((index >= 16) & (index < 19), rest, 0.0),
    )
    return (jnp.concatenate([k, k], axis=0).T, extra.astype(BF).T)


def attend_kernel(mask_ref, q_ref, k_ref, v_ref, ctx_ref, total_ref, keys, values, *, block):
    count = k_ref.shape[1]
    width = q_ref.shape[1]

    @pl.when(pl.program_id(1) == 0)
    def _():
        low, high = extended_keys(k_ref[...], mask_ref[...], False)
        keys[:, :128] = low
        keys[:, 128:] = high
        values[:HEAD_DIM] = v_ref[...]
        values[HEAD_DIM:] = jnp.ones((16, count), BF)

    high, low = scaled_query(q_ref[...])
    query = jnp.concatenate([high, low, jnp.ones((128, width), BF)], axis=0)
    top = jnp.full((1, width), -1e30, F32)
    acc = jnp.zeros((HEAD_DIM + 16, width), F32)
    for j in range(count // block):
        part = pl.ds(j * block, block)
        scores = mm(keys[part, :], query, NN)
        new_top = jnp.maximum(top, jnp.max(scores, axis=0, keepdims=True))
        powers = jnp.exp2(scores - new_top).astype(BF)
        acc = acc * jnp.exp2(top - new_top) + mm(values[:, part], powers, NN)
        top = new_top
    total = acc[HEAD_DIM : HEAD_DIM + 1]
    ctx_ref[...] = (acc[:HEAD_DIM] / total).astype(BF)
    total_ref[...] = (top + jnp.log2(total))[None]


def attend(mask, q, k, v, query_block=3072, block=256):
    width, count = q.shape
    heads = width // HEAD_DIM
    query_block = min(query_block, count)
    q_spec = pl.BlockSpec((HEAD_DIM, query_block), lambda h, i: (h, i))
    k_spec = pl.BlockSpec((HEAD_DIM, count), lambda h, i: (h, 0))
    return pl.pallas_call(
        functools.partial(attend_kernel, block=block),
        grid=(heads, count // query_block),
        in_specs=[pl.BlockSpec((1, count), lambda h, i: (0, 0)), q_spec, k_spec, k_spec],
        out_specs=[q_spec, pl.BlockSpec((1, 1, query_block), lambda h, i: (h, 0, i))],
        out_shape=[
            jax.ShapeDtypeStruct((width, count), BF),
            jax.ShapeDtypeStruct((heads, 1, count), F32),
        ],
        scratch_shapes=[pltpu.VMEM((count, 256), BF), pltpu.VMEM((HEAD_DIM + 16, count), BF)],
        compiler_params=pltpu.CompilerParams(vmem_limit_bytes=VMEM_LIMIT),
        name="attend",
    )(mask, q, k, v)


def attend_back_kernel(
    mask_ref, q_ref, k_ref, v_ref, ctx_ref, g_ref, total_ref,
    dq_ref, dk_ref, dv_ref, keys, values, dk_acc, dv_acc, *, block,
):
    count = k_ref.shape[1]
    width = q_ref.shape[1]

    @pl.when(pl.program_id(1) == 0)
    def _():
        low, high = extended_keys(k_ref[...], mask_ref[...], True)
        keys[:, :128] = low
        keys[:, 128:] = high
        values[...] = jnp.concatenate([v_ref[...], jnp.ones((HEAD_DIM, count), BF)], axis=0).T
        dk_acc[...] = jnp.zeros_like(dk_acc)
        dv_acc[...] = jnp.zeros_like(dv_acc)

    q = q_ref[...]
    g = g_ref[...]
    high, low = scaled_query(q)
    dots = jnp.sum(g.astype(F32) * ctx_ref[...].astype(F32), axis=0, keepdims=True)
    query = jnp.concatenate(
        [high, low, jnp.ones((16, width), BF), row_terms(-total_ref[0], 112, width)], axis=0
    )
    grads = jnp.concatenate([g, row_terms(-dots, HEAD_DIM, width)], axis=0)
    dq = jnp.zeros((HEAD_DIM, width), F32)
    for j in range(count // block):
        part = pl.ds(j * block, block)
        probs = jnp.exp2(mm(keys[part, :], query, NN))
        probs_low = probs.astype(BF)
        grad_scores = (probs * mm(values[part, :], grads, NN)).astype(BF)
        dv_acc[:, part] += mm(g, probs_low, NT)
        dk_acc[:, part] += mm(q, grad_scores, NT)
        dq = dq + mm(k_ref[:, part], grad_scores, NN)
    dq_ref[...] = (dq * HEAD_DIM**-0.5).astype(BF)

    @pl.when(pl.program_id(1) == pl.num_programs(1) - 1)
    def _():
        dk_ref[...] = (dk_acc[...] * HEAD_DIM**-0.5).astype(BF)
        dv_ref[...] = dv_acc[...].astype(BF)


def attend_back(mask, q, k, v, ctx, g, totals, query_block=1024, block=256):
    width, count = q.shape
    heads = width // HEAD_DIM
    q_spec = pl.BlockSpec((HEAD_DIM, query_block), lambda h, i: (h, i))
    k_spec = pl.BlockSpec((HEAD_DIM, count), lambda h, i: (h, 0))
    return pl.pallas_call(
        functools.partial(attend_back_kernel, block=block),
        grid=(heads, count // query_block),
        in_specs=[
            pl.BlockSpec((1, count), lambda h, i: (0, 0)), q_spec, k_spec, k_spec, q_spec, q_spec,
            pl.BlockSpec((1, 1, query_block), lambda h, i: (h, 0, i)),
        ],
        out_specs=[q_spec, k_spec, k_spec],
        out_shape=[jax.ShapeDtypeStruct((width, count), BF)] * 3,
        scratch_shapes=[
            pltpu.VMEM((count, 256), BF),
            pltpu.VMEM((count, 2 * HEAD_DIM), BF),
            pltpu.VMEM((HEAD_DIM, count), F32),
            pltpu.VMEM((HEAD_DIM, count), F32),
        ],
        compiler_params=pltpu.CompilerParams(vmem_limit_bytes=VMEM_LIMIT),
        name="attend_back",
    )(mask, q, k, v, ctx, g, totals)


def middle_kernel(
    count_ref, ctx_ref, in_ref, grad_ref, w_ref, vec_ref,
    out_ref, mixed_grad_ref, ctx_grad_ref, low_sums_ref, rows_ref, sums_ref, outer_ref,
    *, parts, hidden, width,
):
    me = lax.axis_index("mp")
    step = pl.program_id(0)
    block, features = in_ref.shape
    down, outer, tail = features, features + hidden, features + hidden + width
    pieces = w_ref.shape[1]

    def shard(s, start, size):
        low = start // pieces
        return w_ref[s, :, low : low + size // pieces, :].reshape(size, features)


    @pl.when(step == 0)
    def _():
        sums_ref[...] = jnp.zeros_like(sums_ref)
        rows_ref[...] = jnp.zeros_like(rows_ref)
        for s in range(parts):
            outer_ref[s * width : (s + 1) * width, :] = shard(s, outer, width)

    mixed = in_ref[...].astype(F32) + vec_ref[0:1] + mm(ctx_ref[...], outer_ref[...], TN)
    n, inverse = normed(mixed)
    second = (n * vec_ref[1:2] + vec_ref[2:3]).astype(BF)
    row = step * block + lax.broadcasted_iota(jnp.int32, (block, 1), 0)
    grad_y = jnp.where(row < count_ref[0], grad_ref[...].astype(F32), 0.0)
    grad_low = grad_y.astype(BF)
    out = mixed + vec_ref[3:4]
    grad_second = jnp.zeros((block, features), F32)
    for turn in range(parts):
        s = lax.rem(me + turn, parts)
        w_up = shard(s, 0, features)
        w_down = shard(s, down, hidden)
        terms = w_ref[s, 0, tail // pieces : tail // pieces + 8, :].astype(F32)
        up = mm(second, w_up, NN) + (terms[0:1] + terms[1:2] + terms[2:3])
        grad_act = mm(grad_low, w_down, NT)
        below = 0.5 * lax.erf(up * 0.7071067811865476) + 0.5
        density = jnp.exp2(up * up * (-0.5 * LOG2E)) * 0.3989422804014327
        activated = (up * below).astype(BF)
        grad_up = (grad_act * (below + up * density)).astype(BF)
        out = out + mm(activated, w_down, NN)
        grad_second = grad_second + mm(grad_up, w_up, NT)
        if turn == 0:
            sums_ref[0:features, :] += mm(second, grad_up, TN)
            sums_ref[down : down + hidden, :] += mm(activated, grad_low, TN)
            rows_ref[4:5, :] += jnp.sum(
                grad_up.astype(F32), axis=0, keepdims=True
            )
    out_ref[...] = out.astype(BF)
    grad_mixed = grad_y + norm_back(grad_second, n, inverse, vec_ref[1:2])
    mixed_grad_ref[...] = grad_mixed
    mixed_low = grad_mixed.astype(BF)
    own = pl.ds(me * width, width)
    ctx_grad_ref[...] = mm(outer_ref[own, :], mixed_low, NT).astype(BF)
    sums_ref[outer : outer + width, :] += mm(
        ctx_ref[own, :], mixed_low, NN
    )
    rows_ref[0:4, :] += jnp.concatenate(
        [
            jnp.sum(mixed_low.astype(F32), axis=0, keepdims=True),
            jnp.sum(grad_low.astype(F32), axis=0, keepdims=True),
            jnp.sum(grad_second * n, axis=0, keepdims=True),
            jnp.sum(grad_second, axis=0, keepdims=True),
        ],
        axis=0,
    )

    @pl.when(step == pl.num_programs(0) - 1)
    def _():
        low_sums_ref[:tail] = sums_ref[...].astype(BF)
        low_sums_ref[tail:] = jnp.zeros((low_sums_ref.shape[0] - tail, features), BF)


def middle(counts, ctx, rows, grads, weights, vectors, hidden, width, held, block=512):
    count, features = rows.shape
    parts = weights.shape[0]
    row_spec = pl.BlockSpec((block, features), lambda i: (i, 0))
    sums = features + hidden + width
    return pl.pallas_call(
        functools.partial(middle_kernel, parts=parts, hidden=hidden, width=width),
        grid=(count // block,),
        in_specs=[
            pl.BlockSpec(memory_space=pltpu.SMEM),
            pl.BlockSpec((parts * width, block), lambda i: (0, i)),
            row_spec,
            row_spec,
            pl.BlockSpec(weights.shape, lambda i: (0, 0, 0, 0), pipeline_mode=pl.Buffered(1)),
            pl.BlockSpec(vectors.shape, lambda i: (0, 0)),
        ],
        out_specs=[
            row_spec,
            row_spec,
            pl.BlockSpec((width, block), lambda i: (0, i)),
            pl.BlockSpec((held, features), lambda i: (0, 0), pipeline_mode=pl.Buffered(1)),
            pl.BlockSpec((8, features), lambda i: (0, 0)),
        ],
        out_shape=[
            jax.ShapeDtypeStruct((count, features), BF),
            jax.ShapeDtypeStruct((count, features), F32),
            jax.ShapeDtypeStruct((width, count), BF),
            jax.ShapeDtypeStruct((held, features), BF),
            jax.ShapeDtypeStruct((8, features), F32),
        ],
        scratch_shapes=[
            pltpu.VMEM((sums, features), F32), pltpu.VMEM((parts * width, features), BF)
        ],
        compiler_params=pltpu.CompilerParams(vmem_limit_bytes=VMEM_LIMIT),
        name="middle",
    )(counts, ctx, rows, grads, weights, vectors)


def project_back_kernel(
    first_ref, rows_ref, dq_ref, dk_ref, dv_ref, w_ref, small_ref, held_ref,
    part_ref, vec_ref, all_ref, sums_ref, low_ref, sem, *, width, start,
):
    step = pl.program_id(0)

    @pl.when(step == 0)
    def _():
        sums_ref[...] = jnp.zeros_like(sums_ref)
        vec_ref[0:8] = jnp.zeros_like(small_ref)
        vec_ref[8:16] = small_ref[...]
        vec_ref[16:24] = jnp.zeros_like(small_ref)

    grads = jnp.concatenate([dq_ref[...], dk_ref[...], dv_ref[...]], axis=0)
    partial = mm(grads, w_ref[...], TN)
    part_ref[...] = partial.astype(BF)
    n, _ = normed(rows_ref[...].astype(F32))
    vec_ref[0:1] += jnp.sum(partial * n, axis=0, keepdims=True)
    vec_ref[1:2] += jnp.sum(partial, axis=0, keepdims=True)
    sums_ref[...] += mm(grads, first_ref[...], NN)
    ones = jnp.ones((8, grads.shape[1]), BF)
    vec_ref[16:24, : 3 * width] += mm(ones, grads, NT)

    @pl.when(step == pl.num_programs(0) - 1)
    def _():
        low_ref[...] = sums_ref[...].astype(BF)
        copy = pltpu.make_async_copy(low_ref, all_ref.at[pl.ds(start, 3 * width)], sem)
        copy.start()
        copy.wait()


def project_back(first, rows, dq, dk, dv, weight, small, held, start, block=512):
    count, features = first.shape
    width = dq.shape[0]
    row_spec = pl.BlockSpec((block, features), lambda i: (i, 0))
    d_spec = pl.BlockSpec((width, block), lambda i: (0, i))
    whole = lambda t: pl.BlockSpec(t.shape, lambda i: (0, 0))
    return pl.pallas_call(
        functools.partial(project_back_kernel, width=width, start=start),
        grid=(count // block,),
        in_specs=[
            row_spec, row_spec, d_spec, d_spec, d_spec, whole(weight), whole(small),
            pl.BlockSpec(memory_space=pl.ANY),
        ],
        out_specs=[
            row_spec,
            pl.BlockSpec((24, features), lambda i: (0, 0)),
            pl.BlockSpec(memory_space=pl.ANY),
        ],
        out_shape=[
            jax.ShapeDtypeStruct((count, features), BF),
            jax.ShapeDtypeStruct((24, features), F32),
            jax.ShapeDtypeStruct(held.shape, BF),
        ],
        scratch_shapes=[
            pltpu.VMEM((3 * width, features), F32),
            pltpu.VMEM((3 * width, features), BF),
            pltpu.SemaphoreType.DMA,
        ],
        input_output_aliases={7: 2},
        compiler_params=pltpu.CompilerParams(vmem_limit_bytes=VMEM_LIMIT),
        name="project_back",
    )(first, rows, dq, dk, dv, weight, small, held)


def finish_kernel(
    part_ref, all_rows_ref, all_mixed_ref, gain_ref, norm_ref, sums_ref,
    out_ref, total_ref, sum_out,
    rows_ref, mixed_ref, own_sems, from_left, from_right, sum_left, sum_right, sum_send_right, sum_send_left,
    row_left, row_right, row_send_right, row_send_left,
    group_norm, all_norm, sum_in, group_send, group_recv, all_send, all_recv,
    piece_send, piece_recv, done_send, done_recv, *, parts, copies,
):
    me = lax.axis_index("mp")
    chunks = part_ref.shape[1]
    first, last = me == 0, me == parts - 1

    def send(source, target, send_sem, recv_sem, step):
        return pltpu.make_async_remote_copy(
            src_ref=source, dst_ref=target, send_sem=send_sem, recv_sem=recv_sem,
            device_id={"mp": lax.rem(me + step + parts, parts)},
            device_id_type=MESH,
        )

    def sum_copy(k, c, step, source):
        if step > 0:
            return send(source, from_left.at[k - 1, c], sum_send_right.at[k - 1, c], sum_left.at[k - 1, c], 1)
        return send(source, from_right.at[k - 1, c], sum_send_left.at[k - 1, c], sum_right.at[k - 1, c], -1)

    def row_copy(j, c, step):
        owner = lax.rem(me - step * j + parts, parts)
        block = out_ref.at[owner, c]
        if step > 0:
            return send(block, block, row_send_right.at[j, c], row_left.at[j, c], 1)
        return send(block, block, row_send_left.at[j, c], row_right.at[j, c], -1)

    own_copies = (
        pltpu.make_async_copy(all_rows_ref.at[me], rows_ref, own_sems.at[0]),
        pltpu.make_async_copy(all_mixed_ref.at[me], mixed_ref, own_sems.at[1]),
    )
    for copy in own_copies:
        copy.start()
    cell = lax.axis_index("dp")
    small = group_norm.shape[1]

    def to_group(j, source, target, send_sem, recv_sem):
        return pltpu.make_async_remote_copy(
            src_ref=source, dst_ref=target, send_sem=send_sem, recv_sem=recv_sem,
            device_id={"mp": lax.rem(me + j, parts)}, device_id_type=MESH,
        )

    def to_cell(j, source, target, send_sem, recv_sem):
        return pltpu.make_async_remote_copy(
            src_ref=source, dst_ref=target, send_sem=send_sem, recv_sem=recv_sem,
            device_id={"dp": lax.rem(cell + j, copies)}, device_id_type=MESH,
        )

    def group_copy(j, source):
        return to_group(
            j, norm_ref.at[pl.ds(0, small)], group_norm.at[source], group_send.at[j], group_recv.at[source]
        )

    def cell_copy(j, source):
        return to_cell(j, total_ref, all_norm.at[source], all_send.at[j], all_recv.at[source])

    def piece_copy(j, source):
        return to_cell(
            j, sums_ref.at[lax.rem(cell + j, copies)], sum_in.at[source],
            piece_send.at[j], piece_recv.at[source],
        )

    def done_copy(j, source):
        return to_cell(
            j, sum_out.at[source], sum_out.at[source], done_send.at[j], done_recv.at[source]
        )

    def each(then, end):
        lax.fori_loop(1, end, lambda j, carry: (then(j), carry)[1], 0)

    behind = lambda j: lax.rem(cell - j + copies, copies)

    def summed(ref, end):
        return lax.fori_loop(1, end, lambda j, total: total + ref[j], ref[0])

    barrier = pltpu.get_barrier_semaphore()
    each(lambda j: pl.semaphore_signal(
        barrier, inc=1, device_id={"mp": lax.rem(me + j, parts)}, device_id_type=MESH), parts)
    each(lambda j: pl.semaphore_signal(
        barrier, inc=1, device_id={"dp": lax.rem(cell + j, copies)}, device_id_type=MESH), copies)
    pl.semaphore_wait(barrier, parts + copies - 2)
    each(lambda j: group_copy(j, me).start(), parts)
    each(lambda j: piece_copy(j, cell).start(), copies)
    group_norm[me] = norm_ref[0:small]

    def group_total():
        each(lambda j: group_copy(j, lax.rem(me - j + parts, parts)).wait(), parts)
        total_ref[0:small] = summed(group_norm, parts)
        total_ref[small:] = norm_ref[small:]
        all_norm[cell] = total_ref[...]
        each(lambda j: cell_copy(j, cell).start(), copies)

    def piece_total():
        each(lambda j: piece_copy(j, behind(j)).wait(), copies)
        total = lax.fori_loop(
            1, copies, lambda j, total: total + sum_in[behind(j)].astype(F32), sums_ref[cell].astype(F32)
        )
        sum_out[cell] = total.astype(BF)
        each(lambda j: done_copy(j, cell).start(), copies)

    for copy in own_copies:
        copy.wait()

    def pass_sums(step, c):
        place = me if step > 0 else parts - 1 - me
        slots = from_left if step > 0 else from_right
        for k in range(parts - 1, 0, -1):
            owner = lax.rem(me + step * k + parts, parts)

            @pl.when(place == 0)
            def _():
                sum_copy(k, c, step, part_ref.at[owner, c]).start()

            if k < parts - 1:

                @pl.when((place > 0) & (place + k < parts))
                def _():
                    sum_copy(k + 1, c, step, part_ref.at[owner, c]).wait_recv()
                    slots[k, c] = (
                        slots[k, c].astype(F32) + part_ref[owner, c].astype(F32)
                    ).astype(BF)
                    sum_copy(k, c, step, slots.at[k, c]).start()

    def finish(c):
        @pl.when(jnp.logical_not(first))
        def _():
            sum_copy(1, c, 1, part_ref.at[0, c]).wait_recv()

        @pl.when(jnp.logical_not(last))
        def _():
            sum_copy(1, c, -1, part_ref.at[0, c]).wait_recv()

        grad = part_ref[me, c].astype(F32)
        zero = jnp.zeros_like(grad)
        grad = grad + jnp.where(first, zero, from_left[0, c].astype(F32))
        grad = grad + jnp.where(last, zero, from_right[0, c].astype(F32))
        n, inverse = normed(rows_ref[c].astype(F32))
        out_ref[me, c] = (mixed_ref[c] + norm_back(grad, n, inverse, gain_ref[...])).astype(BF)

        @pl.when(jnp.logical_not(last))
        def _():
            row_copy(0, c, 1).start()

        @pl.when(jnp.logical_not(first))
        def _():
            row_copy(0, c, -1).start()

    def pass_rows(step, j, c):
        place = me if step > 0 else parts - 1 - me

        @pl.when(place >= j + 1)
        def _():
            owner = lax.rem(me - step * (j + 1) + 2 * parts, parts)
            block = out_ref.at[owner, c]
            if step > 0:
                arrival = send(block, block, row_send_right.at[j, c], row_left.at[j, c], 1)
            else:
                arrival = send(block, block, row_send_left.at[j, c], row_right.at[j, c], -1)
            arrival.wait_recv()

        if j + 1 < parts - 1:

            @pl.when((place >= j + 1) & (place < parts - 1))
            def _():
                row_copy(j + 1, c, step).start()

    def within(c, then):
        @pl.when((c >= 0) & (c < chunks))
        def _():
            then(c)

    def turn(t, carry):
        within(t - me, lambda c: pass_sums(1, c))
        within(t - (parts - 1 - me), lambda c: pass_sums(-1, c))
        within(t - (parts - 1), finish)
        for j in range(parts - 1):
            within(t - (parts + j), lambda c: pass_rows(1, j, c))
            within(t - (parts + j), lambda c: pass_rows(-1, j, c))

        @pl.when(t == parts)
        def _():
            group_total()

        @pl.when(t == parts + chunks // 2)
        def _():
            piece_total()

        return carry

    lax.fori_loop(0, chunks + 2 * parts - 2, turn, 0)

    def drain(c, carry):
        for step in (1, -1):
            place = me if step > 0 else parts - 1 - me
            for k in range(1, parts):

                @pl.when(place + k < parts)
                def _():
                    sum_copy(k, c, step, part_ref.at[0, c]).wait_send()

            for j in range(parts - 1):

                @pl.when((place >= j) & (place < parts - 1))
                def _():
                    row_copy(j, c, step).wait_send()
        return carry

    lax.fori_loop(0, chunks, drain, 0)
    each(lambda j: cell_copy(j, behind(j)).wait(), copies)
    each(lambda j: done_copy(j, behind(j)).wait(), copies)
    total_ref[...] = summed(all_norm, copies)


def finish(partial, rows, mixed_grad, gain, norm_sums, sums, parts, copies, chunks):
    count, features = partial.shape
    size = count // (parts * chunks)
    whole = (parts, chunks, size, features)
    pieces = (copies, sums.shape[0] // copies, features)
    own = pl.BlockSpec(memory_space=pl.ANY)
    full = pl.BlockSpec(memory_space=pltpu.VMEM)
    dma = pltpu.SemaphoreType.DMA
    return pl.pallas_call(
        functools.partial(finish_kernel, parts=parts, copies=copies),
        in_specs=[full, own, own, full, full, full],
        out_specs=[full, full, full],
        out_shape=[
            jax.ShapeDtypeStruct(whole, BF),
            jax.ShapeDtypeStruct(norm_sums.shape, F32),
            jax.ShapeDtypeStruct(pieces, BF),
        ],
        scratch_shapes=[
            pltpu.VMEM((chunks, size, features), BF),
            pltpu.VMEM((chunks, size, features), F32),
            dma((2,)),
        ]
        + [pltpu.VMEM((parts - 1, chunks, size, features), BF)] * 2
        + [dma((parts - 1, chunks)) for _ in range(8)]
        + [
            pltpu.VMEM((parts, 8, features), F32),
            pltpu.VMEM((copies, *norm_sums.shape), F32),
            pltpu.VMEM(pieces, BF),
        ]
        + [dma((number,)) for number in (parts, parts) + (copies,) * 6],
        compiler_params=pltpu.CompilerParams(
            vmem_limit_bytes=VMEM_LIMIT, collective_id=0, has_side_effects=True
        ),
        name="finish",
    )(
        partial.reshape(whole), rows.reshape(whole), mixed_grad.reshape(whole), gain, norm_sums,
        sums.reshape(pieces),
    )


def per_device(
    inputs, counts, first_gain, first_bias, query_key_value_weight, query_bias, value_bias,
    w_out, out_bias, second_gain, second_bias, w_up, up_bias, w_down, down_bias, out_grad,
):
    _, slots, features = inputs.shape
    width = query_key_value_weight.shape[2]
    hidden = w_up.shape[1]
    parts = lax.axis_size("mp")
    copies = lax.axis_size("dp")
    rows = inputs.reshape(slots, features)
    grads = out_grad.reshape(slots, features)

    bias_terms = jnp.concatenate(
        [jnp.stack(split3(up_bias)), jnp.zeros((5, features), BF)], axis=0
    )
    if width % (8 * copies) == 0 and features % (8 * copies) == 0 and hidden % (8 * copies) == 0:
        pieces = copies
        cut = lambda t: lax.dynamic_slice_in_dim(
            t, lax.axis_index("dp") * (t.shape[0] // copies), t.shape[0] // copies, 0
        )
        piece = jnp.concatenate([cut(w_up), cut(w_down), cut(w_out), bias_terms], axis=0)
    else:
        pieces = 1
        used = features + hidden + width + 8
        padded = -(-used // (16 * copies)) * 16 * copies
        shard = jnp.concatenate(
            [w_up, w_down, w_out, bias_terms, jnp.zeros((padded - used, features), BF)], axis=0
        )
        piece = lax.dynamic_slice_in_dim(
            shard, lax.axis_index("dp") * (padded // copies), padded // copies, 0
        )
    piece, rows = lax.optimization_barrier((piece, rows))
    weights = lax.all_gather(piece, ("mp", "dp"), axis=0, tiled=True)
    weights = weights.reshape(parts, pieces, -1, features)

    weight = query_key_value_weight.transpose(1, 2, 0).reshape(3 * width, features)
    bias = jnp.concatenate([query_bias, jnp.zeros_like(query_bias), value_bias])[:, None]
    first, q, k, v = front(rows, weight, bias, jnp.stack([first_gain, first_bias]))
    mask = jnp.where(jnp.arange(slots)[None, :] < counts[:, None], 0.0, -1e30).astype(F32)
    ctx, totals = attend(mask, q, k, v)
    ctx, weights = lax.optimization_barrier((ctx, weights))
    all_ctx = lax.all_gather(ctx, "mp", axis=0, tiled=True)
    vectors = jnp.stack([out_bias, second_gain, second_bias, down_bias])
    used = features + hidden + 4 * width
    held = -(-used // (16 * copies)) * 16 * copies
    outputs, grad_mixed, ctx_grad, sums, small = middle(
        counts, all_ctx, rows, grads, weights, vectors, hidden, width, held
    )
    dq, dk, dv = attend_back(mask, q, k, v, ctx, ctx_grad, totals)
    late = features + hidden + width
    partial, vec, sums = project_back(first, rows, dq, dk, dv, weight, small, sums, late)
    chunks = next(c for c in (16, 8, 4, 2, 1) if slots % (8 * parts * c) == 0)
    input_grad, vec, sums = finish(
        partial, rows, grad_mixed, first_gain[None], vec, sums, parts, copies, chunks
    )
    sums = sums.reshape(held, features).astype(F32)
    down, outer = features, features + hidden
    return (
        outputs.reshape(inputs.shape),
        input_grad.reshape(inputs.shape).astype(F32),
        vec[0],
        vec[1],
        sums[late : late + 3 * width].reshape(3, width, features).transpose(2, 0, 1),
        vec[16, :width],
        vec[16, 2 * width : 3 * width],
        sums[outer : outer + width],
        vec[8],
        vec[10],
        vec[11],
        sums[:features],
        vec[12],
        sums[down : down + hidden],
        vec[9],
    )


def solution(mesh):
    row = P("dp", None, None)
    return jax.shard_map(
        per_device,
        mesh=mesh,
        in_specs=(
            row, P("dp"), P(), P(), P(None, None, "mp"), P("mp"), P("mp"), P("mp", None), P(),
            P(), P(), P(None, "mp"), P("mp"), P("mp", None), P(), row,
        ),
        out_specs=(
            row, row, P(), P(), P(None, None, "mp"), P("mp"), P("mp"), P("mp", None), P(),
            P(), P(), P(None, "mp"), P("mp"), P("mp", None), P(),
        ),
        check_vma=False,
    )
```

```python
import functools

import jax
import jax.numpy as jnp
from jax import lax
from jax.experimental import pallas as pl
from jax.experimental.pallas import tpu as pltpu
from jax.sharding import PartitionSpec as P

HEAD_DIM = 64
LOG2E = 1.4426950408889634
EPS = 1e-05
BF = jnp.bfloat16
F32 = jnp.float32
NN = (((1,), (0,)), ((), ()))
NT = (((1,), (1,)), ((), ()))
TN = (((0,), (0,)), ((), ()))
VMEM_LIMIT = 62 * 2**20
MESH = pl.DeviceIdType.MESH


def mm(a, b, dims):
    return lax.dot_general(a, b, dims, preferred_element_type=F32)


def split3(v):
    a = v.astype(BF)
    rest = v - a.astype(F32)
    b = rest.astype(BF)
    return (a, b, (rest - b.astype(F32)).astype(BF))


def normed(rows):
    centred = rows - jnp.mean(rows, axis=-1, keepdims=True)
    inverse = lax.rsqrt(jnp.mean(centred * centred, axis=-1, keepdims=True) + EPS)
    return (centred * inverse, inverse)


def norm_back(grad, n, inverse, gain):
    t = grad * gain
    return inverse * (
        t - jnp.mean(t, axis=-1, keepdims=True) - n * jnp.mean(t * n, axis=-1, keepdims=True)
    )


def row_terms(v, count, width):
    a, b, c = split3(v)
    index = lax.broadcasted_iota(jnp.int32, (count, width), 0)
    spread = lambda t: jnp.broadcast_to(t.astype(F32), (count, width))
    zero = jnp.zeros((count, width), F32)
    picked = jnp.where(index == 2, spread(c), zero)
    picked = jnp.where(index == 1, spread(b), picked)
    return jnp.where(index == 0, spread(a), picked).astype(BF)


def front_kernel(in_ref, w_ref, bias_ref, gain_ref, first_ref, q_ref, k_ref, v_ref, *, width):
    n, _ = normed(in_ref[...].astype(F32))
    first = (n * gain_ref[0:1] + gain_ref[1:2]).astype(BF)
    first_ref[...] = first
    projected = mm(w_ref[...], first, NT) + bias_ref[...]
    q_ref[...] = projected[:width].astype(BF)
    k_ref[...] = projected[width : 2 * width].astype(BF)
    v_ref[...] = projected[2 * width :].astype(BF)


def front(rows, weight, bias, gains, block=512):
    count, features = rows.shape
    width = weight.shape[0] // 3
    row_spec = pl.BlockSpec((block, features), lambda i: (i, 0))
    out_spec = pl.BlockSpec((width, block), lambda i: (0, i))
    return pl.pallas_call(
        functools.partial(front_kernel, width=width),
        grid=(count // block,),
        in_specs=[
            row_spec,
            pl.BlockSpec(weight.shape, lambda i: (0, 0)),
            pl.BlockSpec(bias.shape, lambda i: (0, 0)),
            pl.BlockSpec(gains.shape, lambda i: (0, 0)),
        ],
        out_specs=[row_spec, out_spec, out_spec, out_spec],
        out_shape=[jax.ShapeDtypeStruct((count, features), BF)]
        + [jax.ShapeDtypeStruct((width, count), BF)] * 3,
        compiler_params=pltpu.CompilerParams(vmem_limit_bytes=VMEM_LIMIT),
        name="front",
    )(rows, weight, bias, gains)


def scaled_query(q):
    scaled = q.astype(F32) * (LOG2E * HEAD_DIM**-0.5)
    high = scaled.astype(BF)
    return (high, (scaled - high.astype(F32)).astype(BF))


def extended_keys(k, mask, with_ones):
    count = k.shape[1]
    index = lax.broadcasted_iota(jnp.int32, (128, count), 0)
    rest = 1.0 if with_ones else 0.0
    extra = jnp.where(
        index == 0,
        jnp.broadcast_to(mask, (128, count)),
        jnp.where((index >= 16) & (index < 19), rest, 0.0),
    )
    return (jnp.concatenate([k, k], axis=0).T, extra.astype(BF).T)


def attend_kernel(mask_ref, q_ref, k_ref, v_ref, ctx_ref, total_ref, keys, values, *, block):
    count = k_ref.shape[1]
    width = q_ref.shape[1]

    @pl.when(pl.program_id(1) == 0)
    def _():
        low, high = extended_keys(k_ref[...], mask_ref[...], False)
        keys[:, :128] = low
        keys[:, 128:] = high
        values[:HEAD_DIM] = v_ref[...]
        values[HEAD_DIM:] = jnp.ones((16, count), BF)

    high, low = scaled_query(q_ref[...])
    query = jnp.concatenate([high, low, jnp.ones((128, width), BF)], axis=0)
    top = jnp.full((1, width), -1e30, F32)
    acc = jnp.zeros((HEAD_DIM + 16, width), F32)
    for j in range(count // block):
        part = pl.ds(j * block, block)
        scores = mm(keys[part, :], query, NN)
        new_top = jnp.maximum(top, jnp.max(scores, axis=0, keepdims=True))
        powers = jnp.exp2(scores - new_top).astype(BF)
        acc = acc * jnp.exp2(top - new_top) + mm(values[:, part], powers, NN)
        top = new_top
    total = acc[HEAD_DIM : HEAD_DIM + 1]
    ctx = (acc[:HEAD_DIM] / total).astype(BF)
    size = ctx_ref.shape[2]
    for i in range(ctx_ref.shape[0]):
        ctx_ref[i] = ctx[:, i * size : (i + 1) * size]
    total_ref[...] = (top + jnp.log2(total))[None]


def attend(mask, q, k, v, row_block, block=256):
    width, count = q.shape
    heads = width // HEAD_DIM
    head_spec = pl.BlockSpec((HEAD_DIM, count), lambda h, i: (h, 0))
    return pl.pallas_call(
        functools.partial(attend_kernel, block=block),
        grid=(heads, 1),
        in_specs=[pl.BlockSpec((1, count), lambda h, i: (0, 0)), head_spec, head_spec, head_spec],
        out_specs=[
            pl.BlockSpec((count // row_block, HEAD_DIM, row_block), lambda h, i: (0, h, 0)),
            pl.BlockSpec((1, 1, count), lambda h, i: (h, 0, 0)),
        ],
        out_shape=[
            jax.ShapeDtypeStruct((count // row_block, width, row_block), BF),
            jax.ShapeDtypeStruct((heads, 1, count), F32),
        ],
        scratch_shapes=[pltpu.VMEM((count, 256), BF), pltpu.VMEM((HEAD_DIM + 16, count), BF)],
        compiler_params=pltpu.CompilerParams(vmem_limit_bytes=VMEM_LIMIT),
        name="attend",
    )(mask, q, k, v)


def attend_back_kernel(
    mask_ref, q_ref, k_ref, v_ref, g_ref, total_ref, dots_ref,
    dq_ref, dk_ref, dv_ref, keys, values, dk_acc, dv_acc, *, block,
):
    count = k_ref.shape[1]
    width = q_ref.shape[1]

    @pl.when(pl.program_id(1) == 0)
    def _():
        low, high = extended_keys(k_ref[...], mask_ref[...], True)
        keys[:, :128] = low
        keys[:, 128:] = high
        values[...] = jnp.concatenate([v_ref[...], jnp.ones((HEAD_DIM, count), BF)], axis=0).T
        dk_acc[...] = jnp.zeros_like(dk_acc)
        dv_acc[...] = jnp.zeros_like(dv_acc)

    q = q_ref[...]
    g = g_ref[...]
    high, low = scaled_query(q)
    query = jnp.concatenate(
        [high, low, jnp.ones((16, width), BF), row_terms(-total_ref[0], 112, width)], axis=0
    )
    grads = jnp.concatenate([g, row_terms(-dots_ref[0], HEAD_DIM, width)], axis=0)
    dq = jnp.zeros((HEAD_DIM, width), F32)
    for j in range(count // block):
        part = pl.ds(j * block, block)
        probs = jnp.exp2(mm(keys[part, :], query, NN))
        probs_low = probs.astype(BF)
        grad_scores = (probs * mm(values[part, :], grads, NN)).astype(BF)
        dv_acc[:, part] += mm(g, probs_low, NT)
        dk_acc[:, part] += mm(q, grad_scores, NT)
        dq = dq + mm(k_ref[:, part], grad_scores, NN)
    dq_ref[...] = (dq * HEAD_DIM**-0.5).astype(BF)

    @pl.when(pl.program_id(1) == pl.num_programs(1) - 1)
    def _():
        dk_ref[...] = (dk_acc[...] * HEAD_DIM**-0.5).astype(BF)
        dv_ref[...] = dv_acc[...].astype(BF)


def attend_back(mask, q, k, v, g, totals, dots, query_block=1024, block=256):
    width, count = q.shape
    heads = width // HEAD_DIM
    q_spec = pl.BlockSpec((HEAD_DIM, query_block), lambda h, i: (h, i))
    k_spec = pl.BlockSpec((HEAD_DIM, count), lambda h, i: (h, 0))
    return pl.pallas_call(
        functools.partial(attend_back_kernel, block=block),
        grid=(heads, count // query_block),
        in_specs=[
            pl.BlockSpec((1, count), lambda h, i: (0, 0)), q_spec, k_spec, k_spec, q_spec,
            pl.BlockSpec((1, 1, query_block), lambda h, i: (h, 0, i)),
            pl.BlockSpec((1, 1, query_block), lambda h, i: (h, 0, i)),
        ],
        out_specs=[q_spec, k_spec, k_spec],
        out_shape=[jax.ShapeDtypeStruct((width, count), BF)] * 3,
        scratch_shapes=[
            pltpu.VMEM((count, 256), BF),
            pltpu.VMEM((count, 2 * HEAD_DIM), BF),
            pltpu.VMEM((HEAD_DIM, count), F32),
            pltpu.VMEM((HEAD_DIM, count), F32),
        ],
        compiler_params=pltpu.CompilerParams(vmem_limit_bytes=VMEM_LIMIT),
        name="attend_back",
    )(mask, q, k, v, g, totals, dots)


def to_peer(j, source, target, send_sem, recv_sem):
    parts = lax.axis_size("mp")
    return pltpu.make_async_remote_copy(
        src_ref=source, dst_ref=target, send_sem=send_sem, recv_sem=recv_sem,
        device_id={"mp": lax.rem(lax.axis_index("mp") + j, parts)}, device_id_type=MESH,
    )


def meet_group():
    parts = lax.axis_size("mp")
    barrier = pltpu.get_barrier_semaphore()
    for j in range(1, parts):
        pl.semaphore_signal(
            barrier, inc=1, device_id={"mp": lax.rem(lax.axis_index("mp") + j, parts)},
            device_id_type=MESH,
        )
    pl.semaphore_wait(barrier, parts - 1)


def block_copy(own_ref, all_ref, send, recv, j, b, slot, source):
    return to_peer(j, own_ref.at[b], all_ref.at[slot, source], send.at[slot, j], recv.at[slot, source])


def spread_kernel(own_ref, all_ref, send, recv):
    me, parts = lax.axis_index("mp"), lax.axis_size("mp")
    meet_group()
    for b in range(all_ref.shape[0]):
        for j in range(1, parts):
            block_copy(own_ref, all_ref, send, recv, j, b, b, me).start()
    for b in range(all_ref.shape[0]):
        all_ref[b, me] = own_ref[b]
    for b in range(all_ref.shape[0]):
        for j in range(1, parts):
            source = lax.rem(me - j + parts, parts)
            block_copy(own_ref, all_ref, send, recv, j, b, b, source).wait()


def spread(ctx, parts, ahead):
    full = pl.BlockSpec(memory_space=pltpu.VMEM)
    return pl.pallas_call(
        spread_kernel,
        in_specs=[full],
        out_specs=full,
        out_shape=jax.ShapeDtypeStruct((ahead, parts, *ctx.shape[1:]), BF),
        scratch_shapes=[pltpu.SemaphoreType.DMA((ahead, parts))] * 2,
        compiler_params=pltpu.CompilerParams(
            vmem_limit_bytes=VMEM_LIMIT, collective_id=1, has_side_effects=True
        ),
        name="spread",
    )(ctx)


def middle_kernel(
    count_ref, ahead_ref, own_ref, in_ref, grad_ref, w_ref, vec_ref,
    out_ref, mixed_grad_ref, ctx_grad_ref, dots_ref, low_sums_ref, rows_ref,
    sums_ref, outer_ref, ctx_ref, landed_ref, send, recv, *, parts, hidden, width,
):
    me = lax.axis_index("mp")
    step = pl.program_id(0)
    block, features = in_ref.shape
    down, outer, tail = features, features + hidden, features + hidden + width
    pieces = w_ref.shape[1]
    ahead = ahead_ref.shape[0]

    def shard(s, start, size):
        low = start // pieces
        return w_ref[s, :, low : low + size // pieces, :].reshape(size, features)


    @pl.when(step == 0)
    def _():
        sums_ref[...] = jnp.zeros_like(sums_ref)
        rows_ref[...] = jnp.zeros_like(rows_ref)
        for s in range(parts):
            outer_ref[s * width : (s + 1) * width, :] = shard(s, outer, width)
        meet_group()
        for slot in range(landed_ref.shape[0]):
            for j in range(1, parts):
                block_copy(own_ref, landed_ref, send, recv, j, slot + ahead, slot, me).start()

    @pl.when(step < ahead)
    def _():
        for s in range(parts):
            ctx_ref[s * width : (s + 1) * width, :] = ahead_ref[step, s]

    @pl.when(step >= ahead)
    def _():
        for j in range(1, parts):
            source = lax.rem(me - j + parts, parts)
            block_copy(own_ref, landed_ref, send, recv, j, step, step - ahead, source).wait()
        landed_ref[step - ahead, me] = own_ref[step]
        for s in range(parts):
            ctx_ref[s * width : (s + 1) * width, :] = landed_ref[step - ahead, s]

    mixed = in_ref[...].astype(F32) + vec_ref[0:1] + mm(ctx_ref[...], outer_ref[...], TN)
    n, inverse = normed(mixed)
    second = (n * vec_ref[1:2] + vec_ref[2:3]).astype(BF)
    row = step * block + lax.broadcasted_iota(jnp.int32, (block, 1), 0)
    grad_y = jnp.where(row < count_ref[0], grad_ref[...].astype(F32), 0.0)
    grad_low = grad_y.astype(BF)
    out = mixed + vec_ref[3:4]
    grad_second = jnp.zeros((block, features), F32)
    for turn in range(parts):
        s = lax.rem(me + turn, parts)
        w_up = shard(s, 0, features)
        w_down = shard(s, down, hidden)
        terms = w_ref[s, 0, tail // pieces : tail // pieces + 8, :].astype(F32)
        up = mm(second, w_up, NN) + (terms[0:1] + terms[1:2] + terms[2:3])
        grad_act = mm(grad_low, w_down, NT)
        below = 0.5 * lax.erf(up * 0.7071067811865476) + 0.5
        density = jnp.exp2(up * up * (-0.5 * LOG2E)) * 0.3989422804014327
        activated = (up * below).astype(BF)
        grad_up = (grad_act * (below + up * density)).astype(BF)
        out = out + mm(activated, w_down, NN)
        grad_second = grad_second + mm(grad_up, w_up, NT)
        if turn == 0:
            sums_ref[0:features, :] += mm(second, grad_up, TN)
            sums_ref[down : down + hidden, :] += mm(activated, grad_low, TN)
            rows_ref[4:5, :] += jnp.sum(
                grad_up.astype(F32), axis=0, keepdims=True
            )
    out_ref[...] = out.astype(BF)
    grad_mixed = grad_y + norm_back(grad_second, n, inverse, vec_ref[1:2])
    mixed_grad_ref[...] = grad_mixed
    mixed_low = grad_mixed.astype(BF)
    own = pl.ds(me * width, width)
    ctx_grad = mm(outer_ref[own, :], mixed_low, NT).astype(BF)
    ctx_grad_ref[...] = ctx_grad
    products = ctx_grad.astype(F32) * ctx_ref[own, :].astype(F32)
    for h in range(width // HEAD_DIM):
        dots_ref[h] = jnp.sum(products[h * HEAD_DIM : (h + 1) * HEAD_DIM], axis=0, keepdims=True)
    sums_ref[outer : outer + width, :] += mm(
        ctx_ref[own, :], mixed_low, NN
    )
    rows_ref[0:4, :] += jnp.concatenate(
        [
            jnp.sum(mixed_low.astype(F32), axis=0, keepdims=True),
            jnp.sum(grad_low.astype(F32), axis=0, keepdims=True),
            jnp.sum(grad_second * n, axis=0, keepdims=True),
            jnp.sum(grad_second, axis=0, keepdims=True),
        ],
        axis=0,
    )

    @pl.when(step == pl.num_programs(0) - 1)
    def _():
        low_sums_ref[:tail] = sums_ref[...].astype(BF)
        low_sums_ref[tail:] = jnp.zeros((low_sums_ref.shape[0] - tail, features), BF)


def middle(counts, ahead, ctx, rows, grads, weights, vectors, hidden, width, held):
    count, features = rows.shape
    parts = weights.shape[0]
    block = ctx.shape[2]
    rest = ctx.shape[0] - ahead.shape[0]
    row_spec = pl.BlockSpec((block, features), lambda i: (i, 0))
    sums = features + hidden + width
    return pl.pallas_call(
        functools.partial(middle_kernel, parts=parts, hidden=hidden, width=width),
        grid=(count // block,),
        in_specs=[
            pl.BlockSpec(memory_space=pltpu.SMEM),
            pl.BlockSpec(ahead.shape, lambda i: (0, 0, 0, 0), pipeline_mode=pl.Buffered(1)),
            pl.BlockSpec(ctx.shape, lambda i: (0, 0, 0), pipeline_mode=pl.Buffered(1)),
            row_spec,
            row_spec,
            pl.BlockSpec(weights.shape, lambda i: (0, 0, 0, 0), pipeline_mode=pl.Buffered(1)),
            pl.BlockSpec(vectors.shape, lambda i: (0, 0)),
        ],
        out_specs=[
            row_spec,
            row_spec,
            pl.BlockSpec((width, block), lambda i: (0, i)),
            pl.BlockSpec((width // HEAD_DIM, 1, block), lambda i: (0, 0, i)),
            pl.BlockSpec((held, features), lambda i: (0, 0), pipeline_mode=pl.Buffered(1)),
            pl.BlockSpec((8, features), lambda i: (0, 0)),
        ],
        out_shape=[
            jax.ShapeDtypeStruct((count, features), BF),
            jax.ShapeDtypeStruct((count, features), F32),
            jax.ShapeDtypeStruct((width, count), BF),
            jax.ShapeDtypeStruct((width // HEAD_DIM, 1, count), F32),
            jax.ShapeDtypeStruct((held, features), BF),
            jax.ShapeDtypeStruct((8, features), F32),
        ],
        scratch_shapes=[
            pltpu.VMEM((sums, features), F32),
            pltpu.VMEM((parts * width, features), BF),
            pltpu.VMEM((parts * width, block), BF),
            pltpu.VMEM((rest, parts, width, block), BF),
            pltpu.SemaphoreType.DMA((rest, parts)),
            pltpu.SemaphoreType.DMA((rest, parts)),
        ],
        compiler_params=pltpu.CompilerParams(
            vmem_limit_bytes=VMEM_LIMIT, collective_id=2, has_side_effects=True
        ),
        name="middle",
    )(counts, ahead, ctx, rows, grads, weights, vectors)


def project_back_kernel(
    first_ref, rows_ref, dq_ref, dk_ref, dv_ref, w_ref, small_ref, held_ref,
    part_ref, vec_ref, all_ref, sums_ref, low_ref, sem, *, width, start,
):
    step = pl.program_id(0)

    @pl.when(step == 0)
    def _():
        sums_ref[...] = jnp.zeros_like(sums_ref)
        vec_ref[0:8] = jnp.zeros_like(small_ref)
        vec_ref[8:16] = small_ref[...]
        vec_ref[16:24] = jnp.zeros_like(small_ref)

    grads = jnp.concatenate([dq_ref[...], dk_ref[...], dv_ref[...]], axis=0)
    partial = mm(grads, w_ref[...], TN)
    part_ref[...] = partial.astype(BF)
    n, _ = normed(rows_ref[...].astype(F32))
    vec_ref[0:1] += jnp.sum(partial * n, axis=0, keepdims=True)
    vec_ref[1:2] += jnp.sum(partial, axis=0, keepdims=True)
    sums_ref[...] += mm(grads, first_ref[...], NN)
    ones = jnp.ones((8, grads.shape[1]), BF)
    vec_ref[16:24, : 3 * width] += mm(ones, grads, NT)

    @pl.when(step == pl.num_programs(0) - 1)
    def _():
        low_ref[...] = sums_ref[...].astype(BF)
        copy = pltpu.make_async_copy(low_ref, all_ref.at[pl.ds(start, 3 * width)], sem)
        copy.start()
        copy.wait()


def project_back(first, rows, dq, dk, dv, weight, small, held, start, block=512):
    count, features = first.shape
    width = dq.shape[0]
    row_spec = pl.BlockSpec((block, features), lambda i: (i, 0))
    d_spec = pl.BlockSpec((width, block), lambda i: (0, i))
    whole = lambda t: pl.BlockSpec(t.shape, lambda i: (0, 0))
    return pl.pallas_call(
        functools.partial(project_back_kernel, width=width, start=start),
        grid=(count // block,),
        in_specs=[
            row_spec, row_spec, d_spec, d_spec, d_spec, whole(weight), whole(small),
            pl.BlockSpec(memory_space=pl.ANY),
        ],
        out_specs=[
            row_spec,
            pl.BlockSpec((24, features), lambda i: (0, 0)),
            pl.BlockSpec(memory_space=pl.ANY),
        ],
        out_shape=[
            jax.ShapeDtypeStruct((count, features), BF),
            jax.ShapeDtypeStruct((24, features), F32),
            jax.ShapeDtypeStruct(held.shape, BF),
        ],
        scratch_shapes=[
            pltpu.VMEM((3 * width, features), F32),
            pltpu.VMEM((3 * width, features), BF),
            pltpu.SemaphoreType.DMA,
        ],
        input_output_aliases={7: 2},
        compiler_params=pltpu.CompilerParams(vmem_limit_bytes=VMEM_LIMIT),
        name="project_back",
    )(first, rows, dq, dk, dv, weight, small, held)


def finish_kernel(
    part_ref, all_rows_ref, all_mixed_ref, gain_ref, norm_ref, sums_ref,
    out_ref, total_ref, sum_out,
    rows_ref, mixed_ref, own_sems, from_left, from_right, sum_left, sum_right, sum_send_right, sum_send_left,
    row_left, row_right, row_send_right, row_send_left,
    group_norm, all_norm, sum_in, group_send, group_recv, all_send, all_recv,
    piece_send, piece_recv, done_send, done_recv, *, parts, copies,
):
    me = lax.axis_index("mp")
    chunks = part_ref.shape[1]
    first, last = me == 0, me == parts - 1

    def send(source, target, send_sem, recv_sem, step):
        return pltpu.make_async_remote_copy(
            src_ref=source, dst_ref=target, send_sem=send_sem, recv_sem=recv_sem,
            device_id={"mp": lax.rem(me + step + parts, parts)},
            device_id_type=MESH,
        )

    def sum_copy(k, c, step, source):
        if step > 0:
            return send(source, from_left.at[k - 1, c], sum_send_right.at[k - 1, c], sum_left.at[k - 1, c], 1)
        return send(source, from_right.at[k - 1, c], sum_send_left.at[k - 1, c], sum_right.at[k - 1, c], -1)

    def row_copy(j, c, step):
        owner = lax.rem(me - step * j + parts, parts)
        block = out_ref.at[owner, c]
        if step > 0:
            return send(block, block, row_send_right.at[j, c], row_left.at[j, c], 1)
        return send(block, block, row_send_left.at[j, c], row_right.at[j, c], -1)

    own_copies = (
        pltpu.make_async_copy(all_rows_ref.at[me], rows_ref, own_sems.at[0]),
        pltpu.make_async_copy(all_mixed_ref.at[me], mixed_ref, own_sems.at[1]),
    )
    for copy in own_copies:
        copy.start()
    cell = lax.axis_index("dp")
    small = group_norm.shape[1]

    def to_group(j, source, target, send_sem, recv_sem):
        return pltpu.make_async_remote_copy(
            src_ref=source, dst_ref=target, send_sem=send_sem, recv_sem=recv_sem,
            device_id={"mp": lax.rem(me + j, parts)}, device_id_type=MESH,
        )

    def to_cell(j, source, target, send_sem, recv_sem):
        return pltpu.make_async_remote_copy(
            src_ref=source, dst_ref=target, send_sem=send_sem, recv_sem=recv_sem,
            device_id={"dp": lax.rem(cell + j, copies)}, device_id_type=MESH,
        )

    def group_copy(j, source):
        return to_group(
            j, norm_ref.at[pl.ds(0, small)], group_norm.at[source], group_send.at[j], group_recv.at[source]
        )

    def cell_copy(j, source):
        return to_cell(j, total_ref, all_norm.at[source], all_send.at[j], all_recv.at[source])

    def piece_copy(j, source):
        return to_cell(
            j, sums_ref.at[lax.rem(cell + j, copies)], sum_in.at[source],
            piece_send.at[j], piece_recv.at[source],
        )

    def done_copy(j, source):
        return to_cell(
            j, sum_out.at[source], sum_out.at[source], done_send.at[j], done_recv.at[source]
        )

    def each(then, end):
        lax.fori_loop(1, end, lambda j, carry: (then(j), carry)[1], 0)

    behind = lambda j: lax.rem(cell - j + copies, copies)

    def summed(ref, end):
        return lax.fori_loop(1, end, lambda j, total: total + ref[j], ref[0])

    barrier = pltpu.get_barrier_semaphore()
    each(lambda j: pl.semaphore_signal(
        barrier, inc=1, device_id={"mp": lax.rem(me + j, parts)}, device_id_type=MESH), parts)
    each(lambda j: pl.semaphore_signal(
        barrier, inc=1, device_id={"dp": lax.rem(cell + j, copies)}, device_id_type=MESH), copies)
    pl.semaphore_wait(barrier, parts + copies - 2)
    each(lambda j: group_copy(j, me).start(), parts)
    each(lambda j: piece_copy(j, cell).start(), copies)
    group_norm[me] = norm_ref[0:small]

    def group_total():
        each(lambda j: group_copy(j, lax.rem(me - j + parts, parts)).wait(), parts)
        total_ref[0:small] = summed(group_norm, parts)
        total_ref[small:] = norm_ref[small:]
        all_norm[cell] = total_ref[...]
        each(lambda j: cell_copy(j, cell).start(), copies)

    def piece_total():
        each(lambda j: piece_copy(j, behind(j)).wait(), copies)
        total = lax.fori_loop(
            1, copies, lambda j, total: total + sum_in[behind(j)].astype(F32), sums_ref[cell].astype(F32)
        )
        sum_out[cell] = total.astype(BF)
        each(lambda j: done_copy(j, cell).start(), copies)

    for copy in own_copies:
        copy.wait()

    def pass_sums(step, c):
        place = me if step > 0 else parts - 1 - me
        slots = from_left if step > 0 else from_right
        for k in range(parts - 1, 0, -1):
            owner = lax.rem(me + step * k + parts, parts)

            @pl.when(place == 0)
            def _():
                sum_copy(k, c, step, part_ref.at[owner, c]).start()

            if k < parts - 1:

                @pl.when((place > 0) & (place + k < parts))
                def _():
                    sum_copy(k + 1, c, step, part_ref.at[owner, c]).wait_recv()
                    slots[k, c] = (
                        slots[k, c].astype(F32) + part_ref[owner, c].astype(F32)
                    ).astype(BF)
                    sum_copy(k, c, step, slots.at[k, c]).start()

    def finish(c):
        @pl.when(jnp.logical_not(first))
        def _():
            sum_copy(1, c, 1, part_ref.at[0, c]).wait_recv()

        @pl.when(jnp.logical_not(last))
        def _():
            sum_copy(1, c, -1, part_ref.at[0, c]).wait_recv()

        grad = part_ref[me, c].astype(F32)
        zero = jnp.zeros_like(grad)
        grad = grad + jnp.where(first, zero, from_left[0, c].astype(F32))
        grad = grad + jnp.where(last, zero, from_right[0, c].astype(F32))
        n, inverse = normed(rows_ref[c].astype(F32))
        out_ref[me, c] = (mixed_ref[c] + norm_back(grad, n, inverse, gain_ref[...])).astype(BF)

        @pl.when(jnp.logical_not(last))
        def _():
            row_copy(0, c, 1).start()

        @pl.when(jnp.logical_not(first))
        def _():
            row_copy(0, c, -1).start()

    def pass_rows(step, j, c):
        place = me if step > 0 else parts - 1 - me

        @pl.when(place >= j + 1)
        def _():
            owner = lax.rem(me - step * (j + 1) + 2 * parts, parts)
            block = out_ref.at[owner, c]
            if step > 0:
                arrival = send(block, block, row_send_right.at[j, c], row_left.at[j, c], 1)
            else:
                arrival = send(block, block, row_send_left.at[j, c], row_right.at[j, c], -1)
            arrival.wait_recv()

        if j + 1 < parts - 1:

            @pl.when((place >= j + 1) & (place < parts - 1))
            def _():
                row_copy(j + 1, c, step).start()

    def within(c, then):
        @pl.when((c >= 0) & (c < chunks))
        def _():
            then(c)

    def turn(t, carry):
        within(t - me, lambda c: pass_sums(1, c))
        within(t - (parts - 1 - me), lambda c: pass_sums(-1, c))
        within(t - (parts - 1), finish)
        for j in range(parts - 1):
            within(t - (parts + j), lambda c: pass_rows(1, j, c))
            within(t - (parts + j), lambda c: pass_rows(-1, j, c))

        @pl.when(t == parts)
        def _():
            group_total()

        @pl.when(t == parts + chunks // 2)
        def _():
            piece_total()

        return carry

    lax.fori_loop(0, chunks + 2 * parts - 2, turn, 0)

    def drain(c, carry):
        for step in (1, -1):
            place = me if step > 0 else parts - 1 - me
            for k in range(1, parts):

                @pl.when(place + k < parts)
                def _():
                    sum_copy(k, c, step, part_ref.at[0, c]).wait_send()

            for j in range(parts - 1):

                @pl.when((place >= j) & (place < parts - 1))
                def _():
                    row_copy(j, c, step).wait_send()
        return carry

    lax.fori_loop(0, chunks, drain, 0)
    each(lambda j: cell_copy(j, behind(j)).wait(), copies)
    each(lambda j: done_copy(j, behind(j)).wait(), copies)
    total_ref[...] = summed(all_norm, copies)


def finish(partial, rows, mixed_grad, gain, norm_sums, sums, parts, copies, chunks):
    count, features = partial.shape
    size = count // (parts * chunks)
    whole = (parts, chunks, size, features)
    pieces = (copies, sums.shape[0] // copies, features)
    own = pl.BlockSpec(memory_space=pl.ANY)
    full = pl.BlockSpec(memory_space=pltpu.VMEM)
    dma = pltpu.SemaphoreType.DMA
    return pl.pallas_call(
        functools.partial(finish_kernel, parts=parts, copies=copies),
        in_specs=[full, own, own, full, full, full],
        out_specs=[full, full, full],
        out_shape=[
            jax.ShapeDtypeStruct(whole, BF),
            jax.ShapeDtypeStruct(norm_sums.shape, F32),
            jax.ShapeDtypeStruct(pieces, BF),
        ],
        scratch_shapes=[
            pltpu.VMEM((chunks, size, features), BF),
            pltpu.VMEM((chunks, size, features), F32),
            dma((2,)),
        ]
        + [pltpu.VMEM((parts - 1, chunks, size, features), BF)] * 2
        + [dma((parts - 1, chunks)) for _ in range(8)]
        + [
            pltpu.VMEM((parts, 8, features), F32),
            pltpu.VMEM((copies, *norm_sums.shape), F32),
            pltpu.VMEM(pieces, BF),
        ]
        + [dma((number,)) for number in (parts, parts) + (copies,) * 6],
        compiler_params=pltpu.CompilerParams(
            vmem_limit_bytes=VMEM_LIMIT, collective_id=0, has_side_effects=True
        ),
        name="finish",
    )(
        partial.reshape(whole), rows.reshape(whole), mixed_grad.reshape(whole), gain, norm_sums,
        sums.reshape(pieces),
    )


def per_device(
    inputs, counts, first_gain, first_bias, query_key_value_weight, query_bias, value_bias,
    w_out, out_bias, second_gain, second_bias, w_up, up_bias, w_down, down_bias, out_grad,
):
    _, slots, features = inputs.shape
    width = query_key_value_weight.shape[2]
    hidden = w_up.shape[1]
    parts = lax.axis_size("mp")
    copies = lax.axis_size("dp")
    rows = inputs.reshape(slots, features)
    grads = out_grad.reshape(slots, features)

    bias_terms = jnp.concatenate(
        [jnp.stack(split3(up_bias)), jnp.zeros((5, features), BF)], axis=0
    )
    if width % (8 * copies) == 0 and features % (8 * copies) == 0 and hidden % (8 * copies) == 0:
        pieces = copies
        cut = lambda t: lax.dynamic_slice_in_dim(
            t, lax.axis_index("dp") * (t.shape[0] // copies), t.shape[0] // copies, 0
        )
        piece = jnp.concatenate([cut(w_up), cut(w_down), cut(w_out), bias_terms], axis=0)
    else:
        pieces = 1
        used = features + hidden + width + 8
        padded = -(-used // (16 * copies)) * 16 * copies
        shard = jnp.concatenate(
            [w_up, w_down, w_out, bias_terms, jnp.zeros((padded - used, features), BF)], axis=0
        )
        piece = lax.dynamic_slice_in_dim(
            shard, lax.axis_index("dp") * (padded // copies), padded // copies, 0
        )
    piece, rows = lax.optimization_barrier((piece, rows))
    weights = lax.all_gather(piece, ("mp", "dp"), axis=0, tiled=True)
    weights = weights.reshape(parts, pieces, -1, features)

    weight = query_key_value_weight.transpose(1, 2, 0).reshape(3 * width, features)
    bias = jnp.concatenate([query_bias, jnp.zeros_like(query_bias), value_bias])[:, None]
    first, q, k, v = front(rows, weight, bias, jnp.stack([first_gain, first_bias]))
    mask = jnp.where(jnp.arange(slots)[None, :] < counts[:, None], 0.0, -1e30).astype(F32)
    row_block = 512
    ctx, totals = attend(mask, q, k, v, row_block)
    ahead = spread(ctx, parts, slots // row_block // 3)
    vectors = jnp.stack([out_bias, second_gain, second_bias, down_bias])
    used = features + hidden + 4 * width
    held = -(-used // (16 * copies)) * 16 * copies
    outputs, grad_mixed, ctx_grad, dots, sums, small = middle(
        counts, ahead, ctx, rows, grads, weights, vectors, hidden, width, held
    )
    dq, dk, dv = attend_back(mask, q, k, v, ctx_grad, totals, dots)
    late = features + hidden + width
    partial, vec, sums = project_back(first, rows, dq, dk, dv, weight, small, sums, late)
    chunks = next(c for c in (16, 8, 4, 2, 1) if slots % (8 * parts * c) == 0)
    input_grad, vec, sums = finish(
        partial, rows, grad_mixed, first_gain[None], vec, sums, parts, copies, chunks
    )
    sums = sums.reshape(held, features).astype(F32)
    down, outer = features, features + hidden
    return (
        outputs.reshape(inputs.shape),
        input_grad.reshape(inputs.shape).astype(F32),
        vec[0],
        vec[1],
        sums[late : late + 3 * width].reshape(3, width, features).transpose(2, 0, 1),
        vec[16, :width],
        vec[16, 2 * width : 3 * width],
        sums[outer : outer + width],
        vec[8],
        vec[10],
        vec[11],
        sums[:features],
        vec[12],
        sums[down : down + hidden],
        vec[9],
    )


def solution(mesh):
    row = P("dp", None, None)
    return jax.shard_map(
        per_device,
        mesh=mesh,
        in_specs=(
            row, P("dp"), P(), P(), P(None, None, "mp"), P("mp"), P("mp"), P("mp", None), P(),
            P(), P(), P(None, "mp"), P("mp"), P("mp", None), P(), row,
        ),
        out_specs=(
            row, row, P(), P(), P(None, None, "mp"), P("mp"), P("mp"), P("mp", None), P(),
            P(), P(), P(None, "mp"), P("mp"), P("mp", None), P(),
        ),
        check_vma=False,
    )
```

```python
import functools

import jax
import jax.numpy as jnp
from jax import lax
from jax.experimental import pallas as pl
from jax.experimental.pallas import tpu as pltpu
from jax.sharding import PartitionSpec as P

HEAD_DIM = 64
LOG2E = 1.4426950408889634
EPS = 1e-05
BF = jnp.bfloat16
F32 = jnp.float32
NN = (((1,), (0,)), ((), ()))
NT = (((1,), (1,)), ((), ()))
TN = (((0,), (0,)), ((), ()))
VMEM_LIMIT = 62 * 2**20
MESH = pl.DeviceIdType.MESH


def mm(a, b, dims):
    return lax.dot_general(a, b, dims, preferred_element_type=F32)


def split3(v):
    a = v.astype(BF)
    rest = v - a.astype(F32)
    b = rest.astype(BF)
    return (a, b, (rest - b.astype(F32)).astype(BF))


def normed(rows):
    centred = rows - jnp.mean(rows, axis=-1, keepdims=True)
    inverse = lax.rsqrt(jnp.mean(centred * centred, axis=-1, keepdims=True) + EPS)
    return (centred * inverse, inverse)


def norm_back(grad, n, inverse, gain):
    t = grad * gain
    return inverse * (
        t - jnp.mean(t, axis=-1, keepdims=True) - n * jnp.mean(t * n, axis=-1, keepdims=True)
    )


def row_terms(v, count, width):
    a, b, c = split3(v)
    index = lax.broadcasted_iota(jnp.int32, (count, width), 0)
    spread = lambda t: jnp.broadcast_to(t.astype(F32), (count, width))
    zero = jnp.zeros((count, width), F32)
    picked = jnp.where(index == 2, spread(c), zero)
    picked = jnp.where(index == 1, spread(b), picked)
    return jnp.where(index == 0, spread(a), picked).astype(BF)


def front_kernel(in_ref, w_ref, bias_ref, gain_ref, first_ref, q_ref, k_ref, v_ref, *, width):
    n, _ = normed(in_ref[...].astype(F32))
    first = (n * gain_ref[0:1] + gain_ref[1:2]).astype(BF)
    first_ref[...] = first
    projected = mm(w_ref[...], first, NT) + bias_ref[...]
    q_ref[...] = projected[:width].astype(BF)
    k_ref[...] = projected[width : 2 * width].astype(BF)
    v_ref[...] = projected[2 * width :].astype(BF)


def front(rows, weight, bias, gains, block=512):
    count, features = rows.shape
    width = weight.shape[0] // 3
    row_spec = pl.BlockSpec((block, features), lambda i: (i, 0))
    out_spec = pl.BlockSpec((width, block), lambda i: (0, i))
    return pl.pallas_call(
        functools.partial(front_kernel, width=width),
        grid=(count // block,),
        in_specs=[
            row_spec,
            pl.BlockSpec(weight.shape, lambda i: (0, 0)),
            pl.BlockSpec(bias.shape, lambda i: (0, 0)),
            pl.BlockSpec(gains.shape, lambda i: (0, 0)),
        ],
        out_specs=[row_spec, out_spec, out_spec, out_spec],
        out_shape=[jax.ShapeDtypeStruct((count, features), BF)]
        + [jax.ShapeDtypeStruct((width, count), BF)] * 3,
        compiler_params=pltpu.CompilerParams(vmem_limit_bytes=VMEM_LIMIT),
        name="front",
    )(rows, weight, bias, gains)


def scaled_query(q):
    scaled = q.astype(F32) * (LOG2E * HEAD_DIM**-0.5)
    high = scaled.astype(BF)
    return (high, (scaled - high.astype(F32)).astype(BF))


def mask_columns(mask, with_ones):
    count = mask.shape[1]
    index = lax.broadcasted_iota(jnp.int32, (128, count), 0)
    rest = 1.0 if with_ones else 0.0
    extra = jnp.where(
        index == 0,
        jnp.broadcast_to(mask, (128, count)),
        jnp.where((index >= 16) & (index < 19), rest, 0.0),
    )
    return extra.astype(BF).T


def attend_kernel(mask_ref, q_ref, k_ref, v_ref, ctx_ref, total_ref, keys, values, *, block):
    count = k_ref.shape[1]
    width = q_ref.shape[1]

    @pl.when(pl.program_id(1) == 0)
    def _():
        keys[:, :128] = jnp.concatenate([k_ref[...], k_ref[...]], axis=0).T
        keys[:, 128:] = mask_columns(mask_ref[...], False)
        values[:HEAD_DIM] = v_ref[...]
        values[HEAD_DIM:] = jnp.ones((16, count), BF)

    high, low = scaled_query(q_ref[...])
    query = jnp.concatenate([high, low, jnp.ones((128, width), BF)], axis=0)
    top = jnp.full((1, width), -1e30, F32)
    acc = jnp.zeros((HEAD_DIM + 16, width), F32)
    for j in range(count // block):
        part = pl.ds(j * block, block)
        scores = mm(keys[part, :], query, NN)
        new_top = jnp.maximum(top, jnp.max(scores, axis=0, keepdims=True))
        powers = jnp.exp2(scores - new_top).astype(BF)
        acc = acc * jnp.exp2(top - new_top) + mm(values[:, part], powers, NN)
        top = new_top
    total = acc[HEAD_DIM : HEAD_DIM + 1]
    ctx = (acc[:HEAD_DIM] / total).astype(BF)
    size = ctx_ref.shape[2]
    for i in range(ctx_ref.shape[0]):
        ctx_ref[i] = ctx[:, i * size : (i + 1) * size]
    total_ref[...] = (top + jnp.log2(total))[None]


def attend(mask, q, k, v, row_block, block=256):
    width, count = q.shape
    heads = width // HEAD_DIM
    head_spec = pl.BlockSpec((HEAD_DIM, count), lambda h, i: (h, 0))
    return pl.pallas_call(
        functools.partial(attend_kernel, block=block),
        grid=(heads, 1),
        in_specs=[pl.BlockSpec((1, count), lambda h, i: (0, 0)), head_spec, head_spec, head_spec],
        out_specs=[
            pl.BlockSpec((count // row_block, HEAD_DIM, row_block), lambda h, i: (0, h, 0)),
            pl.BlockSpec((1, 1, count), lambda h, i: (h, 0, 0)),
        ],
        out_shape=[
            jax.ShapeDtypeStruct((count // row_block, width, row_block), BF),
            jax.ShapeDtypeStruct((heads, 1, count), F32),
        ],
        scratch_shapes=[pltpu.VMEM((count, 256), BF), pltpu.VMEM((HEAD_DIM + 16, count), BF)],
        compiler_params=pltpu.CompilerParams(vmem_limit_bytes=VMEM_LIMIT),
        name="attend",
    )(mask, q, k, v)


def to_peer(j, source, target, send_sem, recv_sem):
    parts = lax.axis_size("mp")
    return pltpu.make_async_remote_copy(
        src_ref=source, dst_ref=target, send_sem=send_sem, recv_sem=recv_sem,
        device_id={"mp": lax.rem(lax.axis_index("mp") + j, parts)}, device_id_type=MESH,
    )


def meet_group():
    parts = lax.axis_size("mp")
    barrier = pltpu.get_barrier_semaphore()
    for j in range(1, parts):
        pl.semaphore_signal(
            barrier, inc=1, device_id={"mp": lax.rem(lax.axis_index("mp") + j, parts)},
            device_id_type=MESH,
        )
    pl.semaphore_wait(barrier, parts - 1)


def block_copy(own_ref, all_ref, send, recv, j, b, slot, source):
    return to_peer(j, own_ref.at[b], all_ref.at[slot, source], send.at[slot, j], recv.at[slot, source])


def spread_kernel(own_ref, all_ref, send, recv):
    me, parts = lax.axis_index("mp"), lax.axis_size("mp")
    meet_group()
    for b in range(all_ref.shape[0]):
        for j in range(1, parts):
            block_copy(own_ref, all_ref, send, recv, j, b, b, me).start()
    for b in range(all_ref.shape[0]):
        all_ref[b, me] = own_ref[b]
    for b in range(all_ref.shape[0]):
        for j in range(1, parts):
            source = lax.rem(me - j + parts, parts)
            block_copy(own_ref, all_ref, send, recv, j, b, b, source).wait()


def spread(ctx, parts, ahead):
    full = pl.BlockSpec(memory_space=pltpu.VMEM)
    return pl.pallas_call(
        spread_kernel,
        in_specs=[full],
        out_specs=full,
        out_shape=jax.ShapeDtypeStruct((ahead, parts, *ctx.shape[1:]), BF),
        scratch_shapes=[pltpu.SemaphoreType.DMA((ahead, parts))] * 2,
        compiler_params=pltpu.CompilerParams(
            vmem_limit_bytes=VMEM_LIMIT, collective_id=1, has_side_effects=True
        ),
        name="spread",
    )(ctx)


def middle_kernel(
    count_ref, ahead_ref, own_ref, in_ref, grad_ref, w_ref, vec_ref,
    out_ref, mixed_grad_ref, ctx_grad_ref, dots_ref, low_sums_ref, rows_ref,
    sums_ref, outer_ref, ctx_ref, landed_ref, send, recv, *, parts, hidden, width,
):
    me = lax.axis_index("mp")
    step = pl.program_id(0)
    block, features = in_ref.shape
    down, outer, tail = features, features + hidden, features + hidden + width
    pieces = w_ref.shape[1]
    ahead = ahead_ref.shape[0]

    def shard(s, start, size):
        low = start // pieces
        return w_ref[s, :, low : low + size // pieces, :].reshape(size, features)


    @pl.when(step == 0)
    def _():
        sums_ref[...] = jnp.zeros_like(sums_ref)
        rows_ref[...] = jnp.zeros_like(rows_ref)
        for s in range(parts):
            outer_ref[s * width : (s + 1) * width, :] = shard(s, outer, width)
        meet_group()
        for slot in range(landed_ref.shape[0]):
            for j in range(1, parts):
                block_copy(own_ref, landed_ref, send, recv, j, slot + ahead, slot, me).start()

    @pl.when(step < ahead)
    def _():
        for s in range(parts):
            ctx_ref[s * width : (s + 1) * width, :] = ahead_ref[step, s]

    @pl.when(step >= ahead)
    def _():
        for j in range(1, parts):
            source = lax.rem(me - j + parts, parts)
            block_copy(own_ref, landed_ref, send, recv, j, step, step - ahead, source).wait()
        landed_ref[step - ahead, me] = own_ref[step]
        for s in range(parts):
            ctx_ref[s * width : (s + 1) * width, :] = landed_ref[step - ahead, s]

    mixed = in_ref[...].astype(F32) + vec_ref[0:1] + mm(ctx_ref[...], outer_ref[...], TN)
    n, inverse = normed(mixed)
    second = (n * vec_ref[1:2] + vec_ref[2:3]).astype(BF)
    row = step * block + lax.broadcasted_iota(jnp.int32, (block, 1), 0)
    grad_y = jnp.where(row < count_ref[0], grad_ref[...].astype(F32), 0.0)
    grad_low = grad_y.astype(BF)
    out = mixed + vec_ref[3:4]
    grad_second = jnp.zeros((block, features), F32)
    for turn in range(parts):
        s = lax.rem(me + turn, parts)
        w_up = shard(s, 0, features)
        w_down = shard(s, down, hidden)
        terms = w_ref[s, 0, tail // pieces : tail // pieces + 8, :].astype(F32)
        up = mm(second, w_up, NN) + (terms[0:1] + terms[1:2] + terms[2:3])
        grad_act = mm(grad_low, w_down, NT)
        below = 0.5 * lax.erf(up * 0.7071067811865476) + 0.5
        density = jnp.exp2(up * up * (-0.5 * LOG2E)) * 0.3989422804014327
        activated = (up * below).astype(BF)
        grad_up = (grad_act * (below + up * density)).astype(BF)
        out = out + mm(activated, w_down, NN)
        grad_second = grad_second + mm(grad_up, w_up, NT)
        if turn == 0:
            sums_ref[0:features, :] += mm(second, grad_up, TN)
            sums_ref[down : down + hidden, :] += mm(activated, grad_low, TN)
            rows_ref[4:5, :] += jnp.sum(
                grad_up.astype(F32), axis=0, keepdims=True
            )
    out_ref[...] = out.astype(BF)
    grad_mixed = grad_y + norm_back(grad_second, n, inverse, vec_ref[1:2])
    mixed_grad_ref[...] = grad_mixed
    mixed_low = grad_mixed.astype(BF)
    own = pl.ds(me * width, width)
    ctx_grad = mm(outer_ref[own, :], mixed_low, NT).astype(BF)
    ctx_grad_ref[...] = ctx_grad
    products = ctx_grad.astype(F32) * ctx_ref[own, :].astype(F32)
    for h in range(width // HEAD_DIM):
        dots_ref[h] = jnp.sum(products[h * HEAD_DIM : (h + 1) * HEAD_DIM], axis=0, keepdims=True)
    sums_ref[outer : outer + width, :] += mm(
        ctx_ref[own, :], mixed_low, NN
    )
    rows_ref[0:4, :] += jnp.concatenate(
        [
            jnp.sum(mixed_low.astype(F32), axis=0, keepdims=True),
            jnp.sum(grad_low.astype(F32), axis=0, keepdims=True),
            jnp.sum(grad_second * n, axis=0, keepdims=True),
            jnp.sum(grad_second, axis=0, keepdims=True),
        ],
        axis=0,
    )

    @pl.when(step == pl.num_programs(0) - 1)
    def _():
        low_sums_ref[:tail] = sums_ref[...].astype(BF)
        if low_sums_ref.shape[0] > tail:
            low_sums_ref[tail:] = jnp.zeros((low_sums_ref.shape[0] - tail, features), BF)


def middle(counts, ahead, ctx, rows, grads, weights, vectors, hidden, width, held):
    count, features = rows.shape
    parts = weights.shape[0]
    block = ctx.shape[2]
    rest = ctx.shape[0] - ahead.shape[0]
    row_spec = pl.BlockSpec((block, features), lambda i: (i, 0))
    sums = features + hidden + width
    return pl.pallas_call(
        functools.partial(middle_kernel, parts=parts, hidden=hidden, width=width),
        grid=(count // block,),
        in_specs=[
            pl.BlockSpec(memory_space=pltpu.SMEM),
            pl.BlockSpec(ahead.shape, lambda i: (0, 0, 0, 0), pipeline_mode=pl.Buffered(1)),
            pl.BlockSpec(ctx.shape, lambda i: (0, 0, 0), pipeline_mode=pl.Buffered(1)),
            row_spec,
            row_spec,
            pl.BlockSpec(weights.shape, lambda i: (0, 0, 0, 0), pipeline_mode=pl.Buffered(1)),
            pl.BlockSpec(vectors.shape, lambda i: (0, 0)),
        ],
        out_specs=[
            row_spec,
            row_spec,
            pl.BlockSpec((width, block), lambda i: (0, i)),
            pl.BlockSpec((width // HEAD_DIM, 1, block), lambda i: (0, 0, i)),
            pl.BlockSpec((held, features), lambda i: (0, 0), pipeline_mode=pl.Buffered(1)),
            pl.BlockSpec((8, features), lambda i: (0, 0)),
        ],
        out_shape=[
            jax.ShapeDtypeStruct((count, features), BF),
            jax.ShapeDtypeStruct((count, features), F32),
            jax.ShapeDtypeStruct((width, count), BF),
            jax.ShapeDtypeStruct((width // HEAD_DIM, 1, count), F32),
            jax.ShapeDtypeStruct((held, features), BF),
            jax.ShapeDtypeStruct((8, features), F32),
        ],
        scratch_shapes=[
            pltpu.VMEM((sums, features), F32),
            pltpu.VMEM((parts * width, features), BF),
            pltpu.VMEM((parts * width, block), BF),
            pltpu.VMEM((rest, parts, width, block), BF),
            pltpu.SemaphoreType.DMA((rest, parts)),
            pltpu.SemaphoreType.DMA((rest, parts)),
        ],
        compiler_params=pltpu.CompilerParams(
            vmem_limit_bytes=VMEM_LIMIT, collective_id=2, has_side_effects=True
        ),
        name="middle",
    )(counts, ahead, ctx, rows, grads, weights, vectors)


def back_kernel(
    mask_ref, q_ref, k_ref, v_ref, g_ref, total_ref, dots_ref, w_ref, small_ref, gain_ref,
    all_first_ref, all_rows_ref, all_mixed_ref, early_ref,
    out_ref, vec_out, early_out, late_out,
    keys, extra, values, split, terms, dot_terms, dq_acc, dk_acc, dv_acc,
    first_ref, group_rows, block_sems, late_sums, late_ref, vec_ref, total_vec,
    part_ref, rows_ref, mixed_ref, own_early, own_sems, early_in, late_in, from_left, from_right,
    group_norm, all_norm,
    sum_left, sum_right, sum_send_right, sum_send_left,
    row_left, row_right, row_send_right, row_send_left,
    group_send, group_recv, all_send, all_recv,
    early_send, early_recv, early_done_send, early_done_recv,
    late_send, late_recv, late_done_send, late_done_recv, *, parts, copies, block,
):
    me, cell = lax.axis_index("mp"), lax.axis_index("dp")
    groups, _, chunks, size, features = part_ref.shape
    count = q_ref.shape[1]
    width = q_ref.shape[0]
    heads = width // HEAD_DIM
    span = count // groups
    every = groups * chunks
    first, last = me == 0, me == parts - 1
    at = lambda ref, owner, c: ref.at[lax.div(c, chunks), owner, lax.rem(c, chunks)]
    own = lambda ref, c: ref.at[lax.div(c, chunks), lax.rem(c, chunks)]

    def send(source, target, send_sem, recv_sem, step):
        return pltpu.make_async_remote_copy(
            src_ref=source, dst_ref=target, send_sem=send_sem, recv_sem=recv_sem,
            device_id={"mp": lax.rem(me + step + parts, parts)}, device_id_type=MESH,
        )

    def sum_copy(k, c, step, source):
        if step > 0:
            return send(
                source, from_left.at[k - 1, c], sum_send_right.at[k - 1, c], sum_left.at[k - 1, c], 1
            )
        return send(
            source, from_right.at[k - 1, c], sum_send_left.at[k - 1, c], sum_right.at[k - 1, c], -1
        )

    def row_copy(j, c, step, owner):
        rows = at(out_ref, owner, c)
        if step > 0:
            return send(rows, rows, row_send_right.at[j, c], row_left.at[j, c], 1)
        return send(rows, rows, row_send_left.at[j, c], row_right.at[j, c], -1)

    def to_group(j, source, target, send_sem, recv_sem):
        return pltpu.make_async_remote_copy(
            src_ref=source, dst_ref=target, send_sem=send_sem, recv_sem=recv_sem,
            device_id={"mp": lax.rem(me + j, parts)}, device_id_type=MESH,
        )

    def to_cell(j, source, target, send_sem, recv_sem):
        return pltpu.make_async_remote_copy(
            src_ref=source, dst_ref=target, send_sem=send_sem, recv_sem=recv_sem,
            device_id={"dp": lax.rem(cell + j, copies)}, device_id_type=MESH,
        )

    def group_copy(j, source):
        return to_group(
            j, vec_ref, group_norm.at[source], group_send.at[j], group_recv.at[source]
        )

    def cell_copy(j, source):
        return to_cell(j, total_vec, all_norm.at[source], all_send.at[j], all_recv.at[source])

    def early_copy(j, source):
        return to_cell(
            j, early_ref.at[lax.rem(cell + j, copies)], early_in.at[source],
            early_send.at[j], early_recv.at[source],
        )

    def early_done(j, source):
        piece = early_out.at[source]
        return to_cell(j, piece, piece, early_done_send.at[j], early_done_recv.at[source])

    def late_copy(j, source):
        return to_cell(
            j, late_ref.at[lax.rem(cell + j, copies)], late_in.at[source],
            late_send.at[j], late_recv.at[source],
        )

    def late_done(j, source):
        piece = late_out.at[source]
        return to_cell(j, piece, piece, late_done_send.at[j], late_done_recv.at[source])

    def each(then, end):
        lax.fori_loop(1, end, lambda j, carry: (then(j), carry)[1], 0)

    behind = lambda j: lax.rem(cell - j + copies, copies)

    def summed(ref, end):
        return lax.fori_loop(1, end, lambda j, total: total + ref[j], ref[0])

    def added(ref, start):
        return lax.fori_loop(1, copies, lambda j, total: total + ref[behind(j)].astype(F32), start)

    def early_total():
        each(lambda j: early_copy(j, behind(j)).wait(), copies)
        early_out[cell] = added(early_in, own_early[...].astype(F32)).astype(BF)
        each(lambda j: early_done(j, cell).start(), copies)

    def late_total():
        each(lambda j: late_copy(j, behind(j)).wait(), copies)
        late_out[cell] = added(late_in, late_ref[cell].astype(F32)).astype(BF)
        each(lambda j: late_done(j, cell).start(), copies)

    def group_total():
        each(lambda j: group_copy(j, lax.rem(me - j + parts, parts)).wait(), parts)
        index = lax.broadcasted_iota(jnp.int32, total_vec.shape, 0)
        total_vec[...] = jnp.where(index < 2, summed(group_norm, parts), vec_ref[...])
        all_norm[cell] = total_vec[...]
        each(lambda j: cell_copy(j, cell).start(), copies)

    own_copies = [
        pltpu.make_async_copy(early_ref.at[cell], own_early, own_sems.at[0]),
    ]
    for r in range(groups):
        own_copies.append(
            pltpu.make_async_copy(all_rows_ref.at[r, me], rows_ref.at[r], own_sems.at[1 + 2 * r])
        )
        own_copies.append(
            pltpu.make_async_copy(all_mixed_ref.at[r, me], mixed_ref.at[r], own_sems.at[2 + 2 * r])
        )
    for copy in own_copies:
        copy.start()

    def block_copies(r):
        return (
            pltpu.make_async_copy(all_first_ref.at[r], first_ref, block_sems.at[0]),
            pltpu.make_async_copy(all_rows_ref.at[r], group_rows, block_sems.at[1]),
        )

    for copy in block_copies(0):
        copy.start()
    barrier = pltpu.get_barrier_semaphore()
    each(lambda j: pl.semaphore_signal(
        barrier, inc=1, device_id={"mp": lax.rem(me + j, parts)}, device_id_type=MESH), parts)
    each(lambda j: pl.semaphore_signal(
        barrier, inc=1, device_id={"dp": lax.rem(cell + j, copies)}, device_id_type=MESH), copies)
    pl.semaphore_wait(barrier, parts + copies - 2)
    each(lambda j: early_copy(j, cell).start(), copies)

    extra[...] = mask_columns(mask_ref[...], True)
    for h in range(heads):
        head = slice(h * HEAD_DIM, (h + 1) * HEAD_DIM)
        k = k_ref[head, :]
        keys[h] = jnp.concatenate([k, k], axis=0).T
        values[h] = jnp.concatenate([v_ref[head, :], jnp.ones((HEAD_DIM, count), BF)], axis=0).T
        high, low = scaled_query(q_ref[head, :])
        split[h] = jnp.concatenate([high, low], axis=0)
        terms[h] = jnp.concatenate(
            [jnp.ones((16, count), BF), row_terms(-total_ref[h], 16, count)], axis=0
        )
        dot_terms[h] = row_terms(-dots_ref[h], 16, count)
    dq_acc[...] = jnp.zeros_like(dq_acc)
    dk_acc[...] = jnp.zeros_like(dk_acc)
    dv_acc[...] = jnp.zeros_like(dv_acc)
    late_sums[...] = jnp.zeros_like(late_sums)
    vec_ref[...] = jnp.zeros_like(vec_ref)
    vec_ref[2:7] = small_ref[0:5]
    for copy in own_copies:
        copy.wait()

    def pair(h, a, b):
        head = pl.ds(pl.multiple_of(h * HEAD_DIM, HEAD_DIM), HEAD_DIM)
        columns = pl.ds(pl.multiple_of(a * span, block), span)
        q = q_ref[head, columns]
        g = g_ref[head, columns]
        query = jnp.concatenate(
            [split[h, :, columns], terms[h, :, columns], jnp.zeros((96, span), BF)], axis=0
        )
        grads = jnp.concatenate(
            [g, dot_terms[h, :, columns], jnp.zeros((48, span), BF)], axis=0
        )
        dq = jnp.zeros((HEAD_DIM, span), F32)
        for j in range(span // block):
            part = pl.ds(pl.multiple_of(b * span + j * block, block), block)
            key = jnp.concatenate([keys[h, part, :], extra[part, :]], axis=1)
            probs = jnp.exp2(mm(key, query, NN))
            probs_low = probs.astype(BF)
            grad_scores = (probs * mm(values[h, part, :], grads, NN)).astype(BF)
            dv_acc[head, part] += mm(g, probs_low, NT)
            dk_acc[head, part] += mm(q, grad_scores, NT)
            dq = dq + mm(k_ref[head, part], grad_scores, NN)
        dq_acc[head, columns] += dq

    def project(r):
        for copy in block_copies(r):
            copy.wait()
        columns = pl.ds(pl.multiple_of(r * span, block), span)
        grads = jnp.concatenate(
            [
                (dq_acc[:, columns] * HEAD_DIM**-0.5).astype(BF),
                (dk_acc[:, columns] * HEAD_DIM**-0.5).astype(BF),
                dv_acc[:, columns].astype(BF),
            ],
            axis=0,
        )
        partial = mm(grads, w_ref[...], TN)
        part_ref[r] = partial.reshape(parts, chunks, size, features).astype(BF)
        n, _ = normed(group_rows[...].reshape(span, features).astype(F32))
        vec_ref[0:1] += jnp.sum(partial * n, axis=0, keepdims=True)
        vec_ref[1:2] += jnp.sum(partial, axis=0, keepdims=True)
        late_sums[...] += mm(grads, first_ref[...], NN)
        vec_ref[7:8, : 3 * width] += mm(jnp.ones((8, span), BF), grads, NT)[0:1]

        @pl.when(r + 1 < groups)
        def _():
            for copy in block_copies(r + 1):
                copy.start()

    def pass_sums(step, c):
        place = me if step > 0 else parts - 1 - me
        slots = from_left if step > 0 else from_right
        for k in range(parts - 1, 0, -1):
            owner = lax.rem(me + step * k + parts, parts)
            mine = at(part_ref, owner, c)

            @pl.when(place == 0)
            def _():
                sum_copy(k, c, step, mine).start()

            if k < parts - 1:

                @pl.when((place > 0) & (place + k < parts))
                def _():
                    sum_copy(k + 1, c, step, mine).wait_recv()
                    slots[k, c] = (slots[k, c].astype(F32) + mine[...].astype(F32)).astype(BF)
                    sum_copy(k, c, step, slots.at[k, c]).start()

    def complete(c):
        mine = at(part_ref, me, c)

        @pl.when(jnp.logical_not(first))
        def _():
            sum_copy(1, c, 1, mine).wait_recv()

        @pl.when(jnp.logical_not(last))
        def _():
            sum_copy(1, c, -1, mine).wait_recv()

        grad = mine[...].astype(F32)
        zero = jnp.zeros_like(grad)
        grad = grad + jnp.where(first, zero, from_left[0, c].astype(F32))
        grad = grad + jnp.where(last, zero, from_right[0, c].astype(F32))
        n, inverse = normed(own(rows_ref, c)[...].astype(F32))
        at(out_ref, me, c)[...] = (
            own(mixed_ref, c)[...] + norm_back(grad, n, inverse, gain_ref[...])
        ).astype(BF)

        @pl.when(jnp.logical_not(last))
        def _():
            row_copy(0, c, 1, me).start()

        @pl.when(jnp.logical_not(first))
        def _():
            row_copy(0, c, -1, me).start()

    def pass_rows(step, j, c):
        place = me if step > 0 else parts - 1 - me
        owner = lax.rem(me - step * (j + 1) + 2 * parts, parts)

        @pl.when(place >= j + 1)
        def _():
            row_copy(j, c, step, owner).wait_recv()

        if j + 1 < parts - 1:

            @pl.when((place >= j + 1) & (place < parts - 1))
            def _():
                row_copy(j + 1, c, step, owner).start()

    def within(c, then):
        @pl.when((c >= 0) & (c < every))
        def _():
            then(c)

    def turn(t, carry):
        within(t - me, lambda c: pass_sums(1, c))
        within(t - (parts - 1 - me), lambda c: pass_sums(-1, c))
        within(t - (parts - 1), complete)
        for j in range(parts - 1):
            within(t - (parts + j), lambda c: pass_rows(1, j, c))
            within(t - (parts + j), lambda c: pass_rows(-1, j, c))

        @pl.when(t == every)
        def _():
            group_total()
            late_total()

        return carry

    def group(r, carry):
        pairs = (2 * (groups - 1 - r) + 1) * heads

        def work(u, carry):
            p = lax.div(u, heads)
            other = r + lax.div(p + 1, 2)
            odd = lax.rem(p, 2) == 1
            pair(lax.rem(u, heads), lax.select(odd, r, other), lax.select(odd, other, r))
            done = (r - 1) * chunks

            @pl.when(r > 0)
            def _():
                lax.fori_loop(
                    done + lax.div(u * chunks, pairs), done + lax.div((u + 1) * chunks, pairs), turn, 0
                )

            return carry

        lax.fori_loop(0, pairs, work, 0)
        project(r)

        @pl.when(r == groups // 2 - 1)
        def _():
            early_total()

        return carry

    lax.fori_loop(0, groups, group, 0)
    piece = late_ref.shape[1]
    for i in range(copies):
        late_ref[i] = late_sums[i * piece : (i + 1) * piece, :].astype(BF)
    each(lambda j: group_copy(j, me).start(), parts)
    group_norm[me] = vec_ref[...]
    each(lambda j: late_copy(j, cell).start(), copies)
    lax.fori_loop(every - chunks, every + 2 * parts - 2, turn, 0)

    def drain(c, carry):
        for step in (1, -1):
            place = me if step > 0 else parts - 1 - me
            for k in range(1, parts):

                @pl.when(place + k < parts)
                def _():
                    sum_copy(k, c, step, at(part_ref, me, c)).wait_send()

            for j in range(parts - 1):

                @pl.when((place >= j) & (place < parts - 1))
                def _():
                    row_copy(j, c, step, me).wait_send()

        return carry

    lax.fori_loop(0, every, drain, 0)
    each(lambda j: cell_copy(j, behind(j)).wait(), copies)
    each(lambda j: early_done(j, behind(j)).wait(), copies)
    each(lambda j: late_done(j, behind(j)).wait(), copies)
    vec_out[...] = summed(all_norm, copies)


def back(mask, q, k, v, g, totals, dots, weight, small, gain, first, rows, mixed_grad, early,
         parts, copies, groups, chunks, block=256):
    count, features = first.shape
    width = q.shape[0]
    heads = width // HEAD_DIM
    span = count // groups
    size = span // (parts * chunks)
    every = groups * chunks
    whole = (groups, parts, chunks, size, features)
    early_shape = (copies, early.shape[0] // copies, features)
    late_shape = (copies, 3 * width // copies, features)
    hbm = pl.BlockSpec(memory_space=pl.ANY)
    full = pl.BlockSpec(memory_space=pltpu.VMEM)
    dma = pltpu.SemaphoreType.DMA
    vmem = pltpu.VMEM
    return pl.pallas_call(
        functools.partial(back_kernel, parts=parts, copies=copies, block=block),
        in_specs=[full] * 10 + [hbm] * 4,
        out_specs=[full] * 4,
        out_shape=[
            jax.ShapeDtypeStruct(whole, BF),
            jax.ShapeDtypeStruct((8, features), F32),
            jax.ShapeDtypeStruct(early_shape, BF),
            jax.ShapeDtypeStruct(late_shape, BF),
        ],
        scratch_shapes=[
            vmem((heads, count, 2 * HEAD_DIM), BF),
            vmem((count, 128), BF),
            vmem((heads, count, 2 * HEAD_DIM), BF),
            vmem((heads, 2 * HEAD_DIM, count), BF),
            vmem((heads, 32, count), BF),
            vmem((heads, 16, count), BF),
            vmem((width, count), F32),
            vmem((width, count), F32),
            vmem((width, count), F32),
            vmem((span, features), BF),
            vmem(whole[1:], BF),
            dma((2,)),
            vmem((3 * width, features), F32),
            vmem(late_shape, BF),
            vmem((8, features), F32),
            vmem((8, features), F32),
            vmem(whole, BF),
            vmem((groups, chunks, size, features), BF),
            vmem((groups, chunks, size, features), F32),
            vmem(early_shape[1:], BF),
            dma((1 + 2 * groups,)),
            vmem(early_shape, BF),
            vmem(late_shape, BF),
            vmem((parts - 1, every, size, features), BF),
            vmem((parts - 1, every, size, features), BF),
            vmem((parts, 8, features), F32),
            vmem((copies, 8, features), F32),
        ]
        + [dma((parts - 1, every)) for _ in range(8)]
        + [dma((number,)) for number in (parts, parts) + (copies,) * 10],
        compiler_params=pltpu.CompilerParams(
            vmem_limit_bytes=67_000_000, collective_id=0, has_side_effects=True
        ),
        name="back",
    )(
        mask, q, k, v, g, totals, dots, weight, small, gain, first.reshape(groups, span, features),
        rows.reshape(whole), mixed_grad.reshape(whole), early.reshape(early_shape),
    )


def per_device(
    inputs, counts, first_gain, first_bias, query_key_value_weight, query_bias, value_bias,
    w_out, out_bias, second_gain, second_bias, w_up, up_bias, w_down, down_bias, out_grad,
):
    _, slots, features = inputs.shape
    width = query_key_value_weight.shape[2]
    hidden = w_up.shape[1]
    parts = lax.axis_size("mp")
    copies = lax.axis_size("dp")
    rows = inputs.reshape(slots, features)
    grads = out_grad.reshape(slots, features)

    bias_terms = jnp.concatenate(
        [jnp.stack(split3(up_bias)), jnp.zeros((5, features), BF)], axis=0
    )
    if width % (8 * copies) == 0 and features % (8 * copies) == 0 and hidden % (8 * copies) == 0:
        pieces = copies
        cut = lambda t: lax.dynamic_slice_in_dim(
            t, lax.axis_index("dp") * (t.shape[0] // copies), t.shape[0] // copies, 0
        )
        piece = jnp.concatenate([cut(w_up), cut(w_down), cut(w_out), bias_terms], axis=0)
    else:
        pieces = 1
        used = features + hidden + width + 8
        padded = -(-used // (16 * copies)) * 16 * copies
        shard = jnp.concatenate(
            [w_up, w_down, w_out, bias_terms, jnp.zeros((padded - used, features), BF)], axis=0
        )
        piece = lax.dynamic_slice_in_dim(
            shard, lax.axis_index("dp") * (padded // copies), padded // copies, 0
        )
    piece, rows = lax.optimization_barrier((piece, rows))
    weights = lax.all_gather(piece, ("mp", "dp"), axis=0, tiled=True)
    weights = weights.reshape(parts, pieces, -1, features)

    weight = query_key_value_weight.transpose(1, 2, 0).reshape(3 * width, features)
    bias = jnp.concatenate([query_bias, jnp.zeros_like(query_bias), value_bias])[:, None]
    first, q, k, v = front(rows, weight, bias, jnp.stack([first_gain, first_bias]))
    mask = jnp.where(jnp.arange(slots)[None, :] < counts[:, None], 0.0, -1e30).astype(F32)
    row_block = 512
    ctx, totals = attend(mask, q, k, v, row_block)
    ahead = spread(ctx, parts, slots // row_block // 3)
    vectors = jnp.stack([out_bias, second_gain, second_bias, down_bias])
    used = features + hidden + width
    held = -(-used // copies) * copies
    outputs, grad_mixed, ctx_grad, dots, sums, small = middle(
        counts, ahead, ctx, rows, grads, weights, vectors, hidden, width, held
    )
    input_grad, vec, sums, late = back(
        mask, q, k, v, ctx_grad, totals, dots, weight, small, first_gain[None], first, rows,
        grad_mixed, sums, parts, copies, 4, 4,
    )
    sums = sums.reshape(held, features).astype(F32)
    late = late.reshape(3, width, features).astype(F32)
    down, outer = features, features + hidden
    return (
        outputs.reshape(inputs.shape),
        input_grad.reshape(inputs.shape).astype(F32),
        vec[0],
        vec[1],
        late.transpose(2, 0, 1),
        vec[7, :width],
        vec[7, 2 * width : 3 * width],
        sums[outer : outer + width],
        vec[2],
        vec[4],
        vec[5],
        sums[:features],
        vec[6],
        sums[down : down + hidden],
        vec[3],
    )


def solution(mesh):
    row = P("dp", None, None)
    return jax.shard_map(
        per_device,
        mesh=mesh,
        in_specs=(
            row, P("dp"), P(), P(), P(None, None, "mp"), P("mp"), P("mp"), P("mp", None), P(),
            P(), P(), P(None, "mp"), P("mp"), P("mp", None), P(), row,
        ),
        out_specs=(
            row, row, P(), P(), P(None, None, "mp"), P("mp"), P("mp"), P("mp", None), P(),
            P(), P(), P(None, "mp"), P("mp"), P("mp", None), P(),
        ),
        check_vma=False,
    )
```

```python
import functools

import jax
import jax.numpy as jnp
from jax import lax
from jax.experimental import pallas as pl
from jax.experimental.pallas import tpu as pltpu
from jax.sharding import PartitionSpec as P

HEAD_DIM = 64
LOG2E = 1.4426950408889634
EPS = 1e-05
BF = jnp.bfloat16
F32 = jnp.float32
NN = (((1,), (0,)), ((), ()))
NT = (((1,), (1,)), ((), ()))
TN = (((0,), (0,)), ((), ()))
VMEM_LIMIT = 62 * 2**20
MESH = pl.DeviceIdType.MESH


def mm(a, b, dims):
    return lax.dot_general(a, b, dims, preferred_element_type=F32)


def split3(v):
    a = v.astype(BF)
    rest = v - a.astype(F32)
    b = rest.astype(BF)
    return (a, b, (rest - b.astype(F32)).astype(BF))


def normed(rows):
    centred = rows - jnp.mean(rows, axis=-1, keepdims=True)
    inverse = lax.rsqrt(jnp.mean(centred * centred, axis=-1, keepdims=True) + EPS)
    return (centred * inverse, inverse)


def norm_back(grad, n, inverse, gain):
    t = grad * gain
    return inverse * (
        t - jnp.mean(t, axis=-1, keepdims=True) - n * jnp.mean(t * n, axis=-1, keepdims=True)
    )


def row_terms(v, count, width):
    a, b, c = split3(v)
    index = lax.broadcasted_iota(jnp.int32, (count, width), 0)
    spread = lambda t: jnp.broadcast_to(t.astype(F32), (count, width))
    zero = jnp.zeros((count, width), F32)
    picked = jnp.where(index == 2, spread(c), zero)
    picked = jnp.where(index == 1, spread(b), picked)
    return jnp.where(index == 0, spread(a), picked).astype(BF)


def front_kernel(in_ref, w_ref, bias_ref, gain_ref, first_ref, q_ref, k_ref, v_ref, *, width):
    n, _ = normed(in_ref[...].astype(F32))
    first = (n * gain_ref[0:1] + gain_ref[1:2]).astype(BF)
    first_ref[...] = first
    projected = mm(w_ref[...], first, NT) + bias_ref[...]
    q_ref[...] = projected[:width].astype(BF)
    k_ref[...] = projected[width : 2 * width].astype(BF)
    v_ref[...] = projected[2 * width :].astype(BF)


def front(rows, weight, bias, gains, block=512):
    count, features = rows.shape
    width = weight.shape[0] // 3
    row_spec = pl.BlockSpec((block, features), lambda i: (i, 0))
    out_spec = pl.BlockSpec((width, block), lambda i: (0, i))
    return pl.pallas_call(
        functools.partial(front_kernel, width=width),
        grid=(count // block,),
        in_specs=[
            row_spec,
            pl.BlockSpec(weight.shape, lambda i: (0, 0)),
            pl.BlockSpec(bias.shape, lambda i: (0, 0)),
            pl.BlockSpec(gains.shape, lambda i: (0, 0)),
        ],
        out_specs=[row_spec, out_spec, out_spec, out_spec],
        out_shape=[jax.ShapeDtypeStruct((count, features), BF)]
        + [jax.ShapeDtypeStruct((width, count), BF)] * 3,
        compiler_params=pltpu.CompilerParams(vmem_limit_bytes=VMEM_LIMIT),
        name="front",
    )(rows, weight, bias, gains)


def scaled_query(q):
    scaled = q.astype(F32) * (LOG2E * HEAD_DIM**-0.5)
    high = scaled.astype(BF)
    return (high, (scaled - high.astype(F32)).astype(BF))


def mask_columns(mask, with_ones):
    count = mask.shape[1]
    index = lax.broadcasted_iota(jnp.int32, (128, count), 0)
    rest = 1.0 if with_ones else 0.0
    extra = jnp.where(
        index == 0,
        jnp.broadcast_to(mask, (128, count)),
        jnp.where((index >= 16) & (index < 19), rest, 0.0),
    )
    return extra.astype(BF).T


def attend_kernel(mask_ref, q_ref, k_ref, v_ref, ctx_ref, total_ref, keys, values, *, block):
    count = k_ref.shape[1]
    width = q_ref.shape[1]

    @pl.when(pl.program_id(1) == 0)
    def _():
        keys[:, :128] = jnp.concatenate([k_ref[...], k_ref[...]], axis=0).T
        keys[:, 128:] = mask_columns(mask_ref[...], False)
        values[:HEAD_DIM] = v_ref[...]
        values[HEAD_DIM:] = jnp.ones((16, count), BF)

    high, low = scaled_query(q_ref[...])
    query = jnp.concatenate([high, low, jnp.ones((128, width), BF)], axis=0)
    top = jnp.full((1, width), -1e30, F32)
    acc = jnp.zeros((HEAD_DIM + 16, width), F32)
    for j in range(count // block):
        part = pl.ds(j * block, block)
        scores = mm(keys[part, :], query, NN)
        new_top = jnp.maximum(top, jnp.max(scores, axis=0, keepdims=True))
        powers = jnp.exp2(scores - new_top).astype(BF)
        acc = acc * jnp.exp2(top - new_top) + mm(values[:, part], powers, NN)
        top = new_top
    total = acc[HEAD_DIM : HEAD_DIM + 1]
    ctx = (acc[:HEAD_DIM] / total).astype(BF)
    size = ctx_ref.shape[2]
    for i in range(ctx_ref.shape[0]):
        ctx_ref[i] = ctx[:, i * size : (i + 1) * size]
    total_ref[...] = (top + jnp.log2(total))[None]


def attend(mask, q, k, v, row_block, block=256):
    width, count = q.shape
    heads = width // HEAD_DIM
    head_spec = pl.BlockSpec((HEAD_DIM, count), lambda h, i: (h, 0))
    return pl.pallas_call(
        functools.partial(attend_kernel, block=block),
        grid=(heads, 1),
        in_specs=[pl.BlockSpec((1, count), lambda h, i: (0, 0)), head_spec, head_spec, head_spec],
        out_specs=[
            pl.BlockSpec((count // row_block, HEAD_DIM, row_block), lambda h, i: (0, h, 0)),
            pl.BlockSpec((1, 1, count), lambda h, i: (h, 0, 0)),
        ],
        out_shape=[
            jax.ShapeDtypeStruct((count // row_block, width, row_block), BF),
            jax.ShapeDtypeStruct((heads, 1, count), F32),
        ],
        scratch_shapes=[pltpu.VMEM((count, 256), BF), pltpu.VMEM((HEAD_DIM + 16, count), BF)],
        compiler_params=pltpu.CompilerParams(vmem_limit_bytes=VMEM_LIMIT),
        name="attend",
    )(mask, q, k, v)


def to_peer(j, source, target, send_sem, recv_sem):
    parts = lax.axis_size("mp")
    return pltpu.make_async_remote_copy(
        src_ref=source, dst_ref=target, send_sem=send_sem, recv_sem=recv_sem,
        device_id={"mp": lax.rem(lax.axis_index("mp") + j, parts)}, device_id_type=MESH,
    )


def meet_group():
    parts = lax.axis_size("mp")
    barrier = pltpu.get_barrier_semaphore()
    for j in range(1, parts):
        pl.semaphore_signal(
            barrier, inc=1, device_id={"mp": lax.rem(lax.axis_index("mp") + j, parts)},
            device_id_type=MESH,
        )
    pl.semaphore_wait(barrier, parts - 1)


def block_copy(own_ref, all_ref, send, recv, j, b, slot, source):
    return to_peer(j, own_ref.at[b], all_ref.at[slot, source], send.at[slot, j], recv.at[slot, source])


def spread_kernel(
    own_ref, mask_ref, q_ref, k_ref, v_ref, total_ref,
    all_ref, keys, extra, values, split, terms, send_right, send_left, recv_left, recv_right,
):
    me, parts = lax.axis_index("mp"), lax.axis_size("mp")
    count = q_ref.shape[1]
    heads = keys.shape[0]
    blocks = [(b, step) for b in range(all_ref.shape[0]) for step in (1, -1)]
    place = lambda step: me if step > 0 else parts - 1 - me

    def hop(j, b, step, owner):
        target = all_ref.at[b, owner]
        send, recv = (send_right, recv_left) if step > 0 else (send_left, recv_right)
        return to_peer(
            step + parts, own_ref.at[b] if j == 0 else target, target, send.at[j, b], recv.at[j, b]
        )

    meet_group()
    for b, step in blocks:

        @pl.when(place(step) < parts - 1)
        def _():
            hop(0, b, step, me).start()

    for b in range(all_ref.shape[0]):
        all_ref[b, me] = own_ref[b]
    extra[...] = mask_columns(mask_ref[...], True)

    def lay_out(h):
        head = slice(h * HEAD_DIM, (h + 1) * HEAD_DIM)
        k = k_ref[head, :]
        keys[h] = jnp.concatenate([k, k], axis=0).T
        values[h] = jnp.concatenate([v_ref[head, :], jnp.ones((HEAD_DIM, count), BF)], axis=0).T
        split[h] = jnp.concatenate(scaled_query(q_ref[head, :]), axis=0)
        terms[h] = jnp.concatenate(
            [jnp.ones((16, count), BF), row_terms(-total_ref[h], 16, count)], axis=0
        )

    def relay(j):
        for b, step in blocks:
            owner = lax.rem(me - step * (j + 1) + 2 * parts, parts)

            @pl.when(place(step) >= j + 1)
            def _():
                hop(j, b, step, owner).wait_recv()

            if j + 1 < parts - 1:

                @pl.when((place(step) >= j + 1) & (place(step) < parts - 1))
                def _():
                    hop(j + 1, b, step, owner).start()

    for turn in range(max(heads, parts - 1)):
        if turn < heads:
            lay_out(turn)
        if turn < parts - 1:
            relay(turn)
    for j in range(parts - 1):
        for b, step in blocks:

            @pl.when((place(step) >= j) & (place(step) < parts - 1))
            def _():
                hop(j, b, step, me).wait_send()


def spread(ctx, mask, q, k, v, totals, parts, ahead):
    width, count = q.shape
    heads = width // HEAD_DIM
    full = pl.BlockSpec(memory_space=pltpu.VMEM)
    shape = lambda *sizes: jax.ShapeDtypeStruct(sizes, BF)
    return pl.pallas_call(
        spread_kernel,
        in_specs=[full] * 6,
        out_specs=[full] * 6,
        out_shape=[
            shape(ahead, parts, *ctx.shape[1:]),
            shape(heads, count, 2 * HEAD_DIM),
            shape(count, 128),
            shape(heads, count, 2 * HEAD_DIM),
            shape(heads, 2 * HEAD_DIM, count),
            shape(heads, 32, count),
        ],
        scratch_shapes=[pltpu.SemaphoreType.DMA((parts - 1, ahead))] * 4,
        compiler_params=pltpu.CompilerParams(
            vmem_limit_bytes=VMEM_LIMIT, collective_id=1, has_side_effects=True
        ),
        name="spread",
    )(ctx, mask, q, k, v, totals)


def middle_kernel(
    count_ref, ahead_ref, own_ref, in_ref, grad_ref, w_ref, vec_ref,
    out_ref, mixed_grad_ref, ctx_grad_ref, dots_ref, low_sums_ref, rows_ref,
    sums_ref, outer_ref, ctx_ref, landed_ref, send, recv, *, parts, hidden, width,
):
    me = lax.axis_index("mp")
    step = pl.program_id(0)
    block, features = in_ref.shape
    down, outer, tail = features, features + hidden, features + hidden + width
    pieces = w_ref.shape[1]
    ahead = ahead_ref.shape[0]

    def shard(s, start, size):
        low = start // pieces
        return w_ref[s, :, low : low + size // pieces, :].reshape(size, features)


    @pl.when(step == 0)
    def _():
        sums_ref[...] = jnp.zeros_like(sums_ref)
        rows_ref[...] = jnp.zeros_like(rows_ref)
        for s in range(parts):
            outer_ref[s * width : (s + 1) * width, :] = shard(s, outer, width)
        meet_group()
        for slot in range(landed_ref.shape[0]):
            for j in range(1, parts):
                block_copy(own_ref, landed_ref, send, recv, j, slot + ahead, slot, me).start()

    @pl.when(step < ahead)
    def _():
        for s in range(parts):
            ctx_ref[s * width : (s + 1) * width, :] = ahead_ref[step, s]

    @pl.when(step >= ahead)
    def _():
        for j in range(1, parts):
            source = lax.rem(me - j + parts, parts)
            block_copy(own_ref, landed_ref, send, recv, j, step, step - ahead, source).wait()
        landed_ref[step - ahead, me] = own_ref[step]
        for s in range(parts):
            ctx_ref[s * width : (s + 1) * width, :] = landed_ref[step - ahead, s]

    mixed = in_ref[...].astype(F32) + vec_ref[0:1] + mm(ctx_ref[...], outer_ref[...], TN)
    n, inverse = normed(mixed)
    second = (n * vec_ref[1:2] + vec_ref[2:3]).astype(BF)
    row = step * block + lax.broadcasted_iota(jnp.int32, (block, 1), 0)
    grad_y = jnp.where(row < count_ref[0], grad_ref[...].astype(F32), 0.0)
    grad_low = grad_y.astype(BF)
    out = mixed + vec_ref[3:4]
    grad_second = jnp.zeros((block, features), F32)
    for turn in range(parts):
        s = lax.rem(me + turn, parts)
        w_up = shard(s, 0, features)
        w_down = shard(s, down, hidden)
        terms = w_ref[s, 0, tail // pieces : tail // pieces + 8, :].astype(F32)
        up = mm(second, w_up, NN) + (terms[0:1] + terms[1:2] + terms[2:3])
        grad_act = mm(grad_low, w_down, NT)
        below = 0.5 * lax.erf(up * 0.7071067811865476) + 0.5
        density = jnp.exp2(up * up * (-0.5 * LOG2E)) * 0.3989422804014327
        activated = (up * below).astype(BF)
        grad_up = (grad_act * (below + up * density)).astype(BF)
        out = out + mm(activated, w_down, NN)
        grad_second = grad_second + mm(grad_up, w_up, NT)
        if turn == 0:
            sums_ref[0:features, :] += mm(second, grad_up, TN)
            sums_ref[down : down + hidden, :] += mm(activated, grad_low, TN)
            rows_ref[4:5, :] += jnp.sum(
                grad_up.astype(F32), axis=0, keepdims=True
            )
    out_ref[...] = out.astype(BF)
    grad_mixed = grad_y + norm_back(grad_second, n, inverse, vec_ref[1:2])
    mixed_grad_ref[...] = grad_mixed
    mixed_low = grad_mixed.astype(BF)
    own = pl.ds(me * width, width)
    ctx_grad = mm(outer_ref[own, :], mixed_low, NT).astype(BF)
    ctx_grad_ref[...] = ctx_grad
    products = ctx_grad.astype(F32) * ctx_ref[own, :].astype(F32)
    for h in range(width // HEAD_DIM):
        dots_ref[h] = jnp.sum(products[h * HEAD_DIM : (h + 1) * HEAD_DIM], axis=0, keepdims=True)
    sums_ref[outer : outer + width, :] += mm(
        ctx_ref[own, :], mixed_low, NN
    )
    rows_ref[0:4, :] += jnp.concatenate(
        [
            jnp.sum(mixed_low.astype(F32), axis=0, keepdims=True),
            jnp.sum(grad_low.astype(F32), axis=0, keepdims=True),
            jnp.sum(grad_second * n, axis=0, keepdims=True),
            jnp.sum(grad_second, axis=0, keepdims=True),
        ],
        axis=0,
    )

    @pl.when(step == pl.num_programs(0) - 1)
    def _():
        low_sums_ref[:tail] = sums_ref[...].astype(BF)
        if low_sums_ref.shape[0] > tail:
            low_sums_ref[tail:] = jnp.zeros((low_sums_ref.shape[0] - tail, features), BF)


def middle(counts, ahead, ctx, rows, grads, weights, vectors, hidden, width, held):
    count, features = rows.shape
    parts = weights.shape[0]
    block = ctx.shape[2]
    rest = ctx.shape[0] - ahead.shape[0]
    row_spec = pl.BlockSpec((block, features), lambda i: (i, 0))
    sums = features + hidden + width
    return pl.pallas_call(
        functools.partial(middle_kernel, parts=parts, hidden=hidden, width=width),
        grid=(count // block,),
        in_specs=[
            pl.BlockSpec(memory_space=pltpu.SMEM),
            pl.BlockSpec(ahead.shape, lambda i: (0, 0, 0, 0), pipeline_mode=pl.Buffered(1)),
            pl.BlockSpec(ctx.shape, lambda i: (0, 0, 0), pipeline_mode=pl.Buffered(1)),
            row_spec,
            row_spec,
            pl.BlockSpec(weights.shape, lambda i: (0, 0, 0, 0), pipeline_mode=pl.Buffered(1)),
            pl.BlockSpec(vectors.shape, lambda i: (0, 0)),
        ],
        out_specs=[
            row_spec,
            row_spec,
            pl.BlockSpec((width, block), lambda i: (0, i)),
            pl.BlockSpec((width // HEAD_DIM, 1, block), lambda i: (0, 0, i)),
            pl.BlockSpec((held, features), lambda i: (0, 0), pipeline_mode=pl.Buffered(1)),
            pl.BlockSpec((8, features), lambda i: (0, 0)),
        ],
        out_shape=[
            jax.ShapeDtypeStruct((count, features), BF),
            jax.ShapeDtypeStruct((count, features), F32),
            jax.ShapeDtypeStruct((width, count), BF),
            jax.ShapeDtypeStruct((width // HEAD_DIM, 1, count), F32),
            jax.ShapeDtypeStruct((held, features), BF),
            jax.ShapeDtypeStruct((8, features), F32),
        ],
        scratch_shapes=[
            pltpu.VMEM((sums, features), F32),
            pltpu.VMEM((parts * width, features), BF),
            pltpu.VMEM((parts * width, block), BF),
            pltpu.VMEM((rest, parts, width, block), BF),
            pltpu.SemaphoreType.DMA((rest, parts)),
            pltpu.SemaphoreType.DMA((rest, parts)),
        ],
        compiler_params=pltpu.CompilerParams(
            vmem_limit_bytes=VMEM_LIMIT, collective_id=2, has_side_effects=True
        ),
        name="middle",
    )(counts, ahead, ctx, rows, grads, weights, vectors)


def back_kernel(
    q_ref, k_ref, g_ref, keys, extra, values, split, terms, dots_ref, w_ref, small_ref, gain_ref,
    all_first_ref, all_rows_ref, all_mixed_ref, early_ref,
    out_ref, vec_out, early_out, late_out,
    dot_terms, dq_acc, dk_acc, dv_acc,
    first_ref, group_rows, block_sems, late_sums, late_ref, vec_ref, total_vec,
    part_ref, rows_ref, mixed_ref, own_early, own_sems, early_in, late_in, from_left, from_right,
    group_norm, all_norm,
    sum_left, sum_right, sum_send_right, sum_send_left,
    row_left, row_right, row_send_right, row_send_left,
    group_send, group_recv, all_send, all_recv,
    early_send, early_recv, early_done_send, early_done_recv,
    late_send, late_recv, late_done_send, late_done_recv, *, parts, copies, block,
):
    me, cell = lax.axis_index("mp"), lax.axis_index("dp")
    groups, _, chunks, size, features = part_ref.shape
    count = q_ref.shape[1]
    width = q_ref.shape[0]
    heads = width // HEAD_DIM
    span = count // groups
    every = groups * chunks
    first, last = me == 0, me == parts - 1
    at = lambda ref, owner, c: ref.at[lax.div(c, chunks), owner, lax.rem(c, chunks)]
    own = lambda ref, c: ref.at[lax.div(c, chunks), lax.rem(c, chunks)]

    def send(source, target, send_sem, recv_sem, step):
        return pltpu.make_async_remote_copy(
            src_ref=source, dst_ref=target, send_sem=send_sem, recv_sem=recv_sem,
            device_id={"mp": lax.rem(me + step + parts, parts)}, device_id_type=MESH,
        )

    def sum_copy(k, c, step, source):
        if step > 0:
            return send(
                source, from_left.at[k - 1, c], sum_send_right.at[k - 1, c], sum_left.at[k - 1, c], 1
            )
        return send(
            source, from_right.at[k - 1, c], sum_send_left.at[k - 1, c], sum_right.at[k - 1, c], -1
        )

    def row_copy(j, c, step, owner):
        rows = at(out_ref, owner, c)
        if step > 0:
            return send(rows, rows, row_send_right.at[j, c], row_left.at[j, c], 1)
        return send(rows, rows, row_send_left.at[j, c], row_right.at[j, c], -1)

    def to_group(j, source, target, send_sem, recv_sem):
        return pltpu.make_async_remote_copy(
            src_ref=source, dst_ref=target, send_sem=send_sem, recv_sem=recv_sem,
            device_id={"mp": lax.rem(me + j, parts)}, device_id_type=MESH,
        )

    def to_cell(j, source, target, send_sem, recv_sem):
        return pltpu.make_async_remote_copy(
            src_ref=source, dst_ref=target, send_sem=send_sem, recv_sem=recv_sem,
            device_id={"dp": lax.rem(cell + j, copies)}, device_id_type=MESH,
        )

    def group_copy(j, source):
        return to_group(
            j, vec_ref, group_norm.at[source], group_send.at[j], group_recv.at[source]
        )

    def cell_copy(j, source):
        return to_cell(j, total_vec, all_norm.at[source], all_send.at[j], all_recv.at[source])

    def early_copy(j, source):
        return to_cell(
            j, early_ref.at[lax.rem(cell + j, copies)], early_in.at[source],
            early_send.at[j], early_recv.at[source],
        )

    def early_done(j, source):
        piece = early_out.at[source]
        return to_cell(j, piece, piece, early_done_send.at[j], early_done_recv.at[source])

    def late_copy(j, source):
        return to_cell(
            j, late_ref.at[lax.rem(cell + j, copies)], late_in.at[source],
            late_send.at[j], late_recv.at[source],
        )

    def late_done(j, source):
        piece = late_out.at[source]
        return to_cell(j, piece, piece, late_done_send.at[j], late_done_recv.at[source])

    def each(then, end):
        lax.fori_loop(1, end, lambda j, carry: (then(j), carry)[1], 0)

    behind = lambda j: lax.rem(cell - j + copies, copies)

    def summed(ref, end):
        return lax.fori_loop(1, end, lambda j, total: total + ref[j], ref[0])

    def added(ref, start):
        return lax.fori_loop(1, copies, lambda j, total: total + ref[behind(j)].astype(F32), start)

    def early_total():
        each(lambda j: early_copy(j, behind(j)).wait(), copies)
        early_out[cell] = added(early_in, own_early[...].astype(F32)).astype(BF)
        each(lambda j: early_done(j, cell).start(), copies)

    def late_total():
        each(lambda j: late_copy(j, behind(j)).wait(), copies)
        late_out[cell] = added(late_in, late_ref[cell].astype(F32)).astype(BF)
        each(lambda j: late_done(j, cell).start(), copies)

    def group_total():
        each(lambda j: group_copy(j, lax.rem(me - j + parts, parts)).wait(), parts)
        index = lax.broadcasted_iota(jnp.int32, total_vec.shape, 0)
        total_vec[...] = jnp.where(index < 2, summed(group_norm, parts), vec_ref[...])
        all_norm[cell] = total_vec[...]
        each(lambda j: cell_copy(j, cell).start(), copies)

    own_copies = [
        pltpu.make_async_copy(early_ref.at[cell], own_early, own_sems.at[0]),
    ]
    for r in range(groups):
        own_copies.append(
            pltpu.make_async_copy(all_rows_ref.at[r, me], rows_ref.at[r], own_sems.at[1 + 2 * r])
        )
        own_copies.append(
            pltpu.make_async_copy(all_mixed_ref.at[r, me], mixed_ref.at[r], own_sems.at[2 + 2 * r])
        )
    for copy in own_copies:
        copy.start()

    def block_copies(r):
        return (
            pltpu.make_async_copy(all_first_ref.at[r], first_ref, block_sems.at[0]),
            pltpu.make_async_copy(all_rows_ref.at[r], group_rows, block_sems.at[1]),
        )

    for copy in block_copies(0):
        copy.start()
    barrier = pltpu.get_barrier_semaphore()
    each(lambda j: pl.semaphore_signal(
        barrier, inc=1, device_id={"mp": lax.rem(me + j, parts)}, device_id_type=MESH), parts)
    each(lambda j: pl.semaphore_signal(
        barrier, inc=1, device_id={"dp": lax.rem(cell + j, copies)}, device_id_type=MESH), copies)
    pl.semaphore_wait(barrier, parts + copies - 2)
    each(lambda j: early_copy(j, cell).start(), copies)

    for h in range(heads):
        dot_terms[h] = row_terms(-dots_ref[h], 16, count)
    dq_acc[...] = jnp.zeros_like(dq_acc)
    dk_acc[...] = jnp.zeros_like(dk_acc)
    dv_acc[...] = jnp.zeros_like(dv_acc)
    late_sums[...] = jnp.zeros_like(late_sums)
    vec_ref[...] = jnp.zeros_like(vec_ref)
    vec_ref[2:7] = small_ref[0:5]
    for copy in own_copies:
        copy.wait()

    def pair(h, a, b):
        head = slice(h * HEAD_DIM, (h + 1) * HEAD_DIM)
        columns = pl.ds(pl.multiple_of(a * span, block), span)
        q = q_ref[head, columns]
        g = g_ref[head, columns]
        query = jnp.concatenate(
            [split[h, :, columns], terms[h, :, columns], jnp.zeros((96, span), BF)], axis=0
        )
        grads = jnp.concatenate(
            [g, dot_terms[h, :, columns], jnp.zeros((48, span), BF)], axis=0
        )
        dq = jnp.zeros((HEAD_DIM, span), F32)
        for j in range(span // block):
            part = pl.ds(pl.multiple_of(b * span + j * block, block), block)
            key = jnp.concatenate([keys[h, part, :], extra[part, :]], axis=1)
            probs = jnp.exp2(mm(key, query, NN))
            probs_low = probs.astype(BF)
            grad_scores = (probs * mm(values[h, part, :], grads, NN)).astype(BF)
            dv_acc[head, part] += mm(g, probs_low, NT)
            dk_acc[head, part] += mm(q, grad_scores, NT)
            dq = dq + mm(k_ref[head, part], grad_scores, NN)
        dq_acc[head, columns] += dq

    def project(r):
        for copy in block_copies(r):
            copy.wait()
        columns = pl.ds(pl.multiple_of(r * span, block), span)
        grads = jnp.concatenate(
            [
                (dq_acc[:, columns] * HEAD_DIM**-0.5).astype(BF),
                (dk_acc[:, columns] * HEAD_DIM**-0.5).astype(BF),
                dv_acc[:, columns].astype(BF),
            ],
            axis=0,
        )
        partial = mm(grads, w_ref[...], TN)
        part_ref[r] = partial.reshape(parts, chunks, size, features).astype(BF)
        n, _ = normed(group_rows[...].reshape(span, features).astype(F32))
        vec_ref[0:1] += jnp.sum(partial * n, axis=0, keepdims=True)
        vec_ref[1:2] += jnp.sum(partial, axis=0, keepdims=True)
        late_sums[...] += mm(grads, first_ref[...], NN)
        vec_ref[7:8, : 3 * width] += mm(jnp.ones((8, span), BF), grads, NT)[0:1]

        @pl.when(r + 1 < groups)
        def _():
            for copy in block_copies(r + 1):
                copy.start()

    def start_sums(c, carry):
        for step in (1, -1):
            place = me if step > 0 else parts - 1 - me
            for k in range(parts - 1, 0, -1):
                owner = lax.rem(me + step * k + parts, parts)

                @pl.when(place == 0)
                def _():
                    sum_copy(k, c, step, at(part_ref, owner, c)).start()

    def pass_sums(step, c):
        place = me if step > 0 else parts - 1 - me
        slots = from_left if step > 0 else from_right
        for k in range(parts - 2, 0, -1):
            owner = lax.rem(me + step * k + parts, parts)
            mine = at(part_ref, owner, c)

            @pl.when((place > 0) & (place + k < parts))
            def _():
                sum_copy(k + 1, c, step, mine).wait_recv()
                slots[k, c] = (slots[k, c].astype(F32) + mine[...].astype(F32)).astype(BF)
                sum_copy(k, c, step, slots.at[k, c]).start()

    def complete(c):
        mine = at(part_ref, me, c)

        @pl.when(jnp.logical_not(first))
        def _():
            sum_copy(1, c, 1, mine).wait_recv()

        @pl.when(jnp.logical_not(last))
        def _():
            sum_copy(1, c, -1, mine).wait_recv()

        grad = mine[...].astype(F32)
        zero = jnp.zeros_like(grad)
        grad = grad + jnp.where(first, zero, from_left[0, c].astype(F32))
        grad = grad + jnp.where(last, zero, from_right[0, c].astype(F32))
        n, inverse = normed(own(rows_ref, c)[...].astype(F32))
        at(out_ref, me, c)[...] = (
            own(mixed_ref, c)[...] + norm_back(grad, n, inverse, gain_ref[...])
        ).astype(BF)

        @pl.when(jnp.logical_not(last))
        def _():
            row_copy(0, c, 1, me).start()

        @pl.when(jnp.logical_not(first))
        def _():
            row_copy(0, c, -1, me).start()

    def pass_rows(step, j, c):
        place = me if step > 0 else parts - 1 - me
        owner = lax.rem(me - step * (j + 1) + 2 * parts, parts)

        @pl.when(place >= j + 1)
        def _():
            row_copy(j, c, step, owner).wait_recv()

        if j + 1 < parts - 1:

            @pl.when((place >= j + 1) & (place < parts - 1))
            def _():
                row_copy(j + 1, c, step, owner).start()

    def within(c, then):
        @pl.when((c >= 0) & (c < every))
        def _():
            then(c)

    def turn(t, carry):
        within(t, lambda c: start_sums(c, 0))
        within(t - me, lambda c: pass_sums(1, c))
        within(t - (parts - 1 - me), lambda c: pass_sums(-1, c))
        within(t - (parts - 1), complete)
        for j in range(parts - 1):
            within(t - (parts + j), lambda c: pass_rows(1, j, c))
            within(t - (parts + j), lambda c: pass_rows(-1, j, c))

        @pl.when(t == every)
        def _():
            group_total()
            late_total()

        return carry

    def group(r, carry):
        pairs = 2 * (groups - 1 - r) + 1

        def work(p, carry):
            other = r + lax.div(p + 1, 2)
            odd = lax.rem(p, 2) == 1
            for h in range(heads):
                pair(h, lax.select(odd, r, other), lax.select(odd, other, r))
            done = (r - 1) * chunks

            @pl.when(r > 0)
            def _():
                lax.fori_loop(
                    done + lax.div(p * chunks + pairs - 1, pairs), done + lax.div((p + 1) * chunks + pairs - 1, pairs), turn, 0
                )

            return carry

        lax.fori_loop(0, pairs, work, 0)
        project(r)

        @pl.when(r == groups // 2 - 1)
        def _():
            early_total()

        return carry

    lax.fori_loop(0, groups, group, 0)
    piece = late_ref.shape[1]
    for i in range(copies):
        late_ref[i] = late_sums[i * piece : (i + 1) * piece, :].astype(BF)
    each(lambda j: group_copy(j, me).start(), parts)
    group_norm[me] = vec_ref[...]
    each(lambda j: late_copy(j, cell).start(), copies)
    lax.fori_loop(every - chunks, every + 2 * parts - 2, turn, 0)

    def drain(c, carry):
        for step in (1, -1):
            place = me if step > 0 else parts - 1 - me
            for k in range(1, parts):

                @pl.when(place + k < parts)
                def _():
                    sum_copy(k, c, step, at(part_ref, me, c)).wait_send()

            for j in range(parts - 1):

                @pl.when((place >= j) & (place < parts - 1))
                def _():
                    row_copy(j, c, step, me).wait_send()

        return carry

    lax.fori_loop(0, every, drain, 0)
    each(lambda j: cell_copy(j, behind(j)).wait(), copies)
    each(lambda j: early_done(j, behind(j)).wait(), copies)
    each(lambda j: late_done(j, behind(j)).wait(), copies)
    vec_out[...] = summed(all_norm, copies)


def back(q, k, g, operands, dots, weight, small, gain, first, rows, mixed_grad, early, parts,
         copies, groups, chunks, block=256):
    count, features = first.shape
    width = q.shape[0]
    heads = width // HEAD_DIM
    span = count // groups
    size = span // (parts * chunks)
    every = groups * chunks
    whole = (groups, parts, chunks, size, features)
    early_shape = (copies, early.shape[0] // copies, features)
    late_shape = (copies, 3 * width // copies, features)
    hbm = pl.BlockSpec(memory_space=pl.ANY)
    full = pl.BlockSpec(memory_space=pltpu.VMEM)
    dma = pltpu.SemaphoreType.DMA
    vmem = pltpu.VMEM
    return pl.pallas_call(
        functools.partial(back_kernel, parts=parts, copies=copies, block=block),
        in_specs=[full] * 12 + [hbm] * 4,
        out_specs=[full] * 4,
        out_shape=[
            jax.ShapeDtypeStruct(whole, BF),
            jax.ShapeDtypeStruct((8, features), F32),
            jax.ShapeDtypeStruct(early_shape, BF),
            jax.ShapeDtypeStruct(late_shape, BF),
        ],
        scratch_shapes=[
            vmem((heads, 16, count), BF),
            vmem((width, count), F32),
            vmem((width, count), F32),
            vmem((width, count), F32),
            vmem((span, features), BF),
            vmem(whole[1:], BF),
            dma((2,)),
            vmem((3 * width, features), F32),
            vmem(late_shape, BF),
            vmem((8, features), F32),
            vmem((8, features), F32),
            vmem(whole, BF),
            vmem((groups, chunks, size, features), BF),
            vmem((groups, chunks, size, features), F32),
            vmem(early_shape[1:], BF),
            dma((1 + 2 * groups,)),
            vmem(early_shape, BF),
            vmem(late_shape, BF),
            vmem((parts - 1, every, size, features), BF),
            vmem((parts - 1, every, size, features), BF),
            vmem((parts, 8, features), F32),
            vmem((copies, 8, features), F32),
        ]
        + [dma((parts - 1, every)) for _ in range(8)]
        + [dma((number,)) for number in (parts, parts) + (copies,) * 10],
        compiler_params=pltpu.CompilerParams(
            vmem_limit_bytes=67_000_000, collective_id=0, has_side_effects=True
        ),
        name="back",
    )(
        q, k, g, *operands, dots, weight, small, gain, first.reshape(groups, span, features),
        rows.reshape(whole), mixed_grad.reshape(whole), early.reshape(early_shape),
    )


def per_device(
    inputs, counts, first_gain, first_bias, query_key_value_weight, query_bias, value_bias,
    w_out, out_bias, second_gain, second_bias, w_up, up_bias, w_down, down_bias, out_grad,
):
    _, slots, features = inputs.shape
    width = query_key_value_weight.shape[2]
    hidden = w_up.shape[1]
    parts = lax.axis_size("mp")
    copies = lax.axis_size("dp")
    rows = inputs.reshape(slots, features)
    grads = out_grad.reshape(slots, features)

    bias_terms = jnp.concatenate(
        [jnp.stack(split3(up_bias)), jnp.zeros((5, features), BF)], axis=0
    )
    if width % (8 * copies) == 0 and features % (8 * copies) == 0 and hidden % (8 * copies) == 0:
        pieces = copies
        cut = lambda t: lax.dynamic_slice_in_dim(
            t, lax.axis_index("dp") * (t.shape[0] // copies), t.shape[0] // copies, 0
        )
        piece = jnp.concatenate([cut(w_up), cut(w_down), cut(w_out), bias_terms], axis=0)
    else:
        pieces = 1
        used = features + hidden + width + 8
        padded = -(-used // (16 * copies)) * 16 * copies
        shard = jnp.concatenate(
            [w_up, w_down, w_out, bias_terms, jnp.zeros((padded - used, features), BF)], axis=0
        )
        piece = lax.dynamic_slice_in_dim(
            shard, lax.axis_index("dp") * (padded // copies), padded // copies, 0
        )
    piece, rows = lax.optimization_barrier((piece, rows))
    weights = lax.all_gather(piece, ("mp", "dp"), axis=0, tiled=True)
    weights = weights.reshape(parts, pieces, -1, features)

    weight = query_key_value_weight.transpose(1, 2, 0).reshape(3 * width, features)
    bias = jnp.concatenate([query_bias, jnp.zeros_like(query_bias), value_bias])[:, None]
    first, q, k, v = front(rows, weight, bias, jnp.stack([first_gain, first_bias]))
    mask = jnp.where(jnp.arange(slots)[None, :] < counts[:, None], 0.0, -1e30).astype(F32)
    row_block = 512
    ctx, totals = attend(mask, q, k, v, row_block)
    ahead, *operands = spread(ctx, mask, q, k, v, totals, parts, slots // row_block // 3)
    vectors = jnp.stack([out_bias, second_gain, second_bias, down_bias])
    used = features + hidden + width
    held = -(-used // copies) * copies
    outputs, grad_mixed, ctx_grad, dots, sums, small = middle(
        counts, ahead, ctx, rows, grads, weights, vectors, hidden, width, held
    )
    input_grad, vec, sums, late = back(
        q, k, ctx_grad, operands, dots, weight, small, first_gain[None], first, rows, grad_mixed,
        sums, parts, copies, 4, 4,
    )
    sums = sums.reshape(held, features).astype(F32)
    late = late.reshape(3, width, features).astype(F32)
    down, outer = features, features + hidden
    return (
        outputs.reshape(inputs.shape),
        input_grad.reshape(inputs.shape).astype(F32),
        vec[0],
        vec[1],
        late.transpose(2, 0, 1),
        vec[7, :width],
        vec[7, 2 * width : 3 * width],
        sums[outer : outer + width],
        vec[2],
        vec[4],
        vec[5],
        sums[:features],
        vec[6],
        sums[down : down + hidden],
        vec[3],
    )


def solution(mesh):
    row = P("dp", None, None)
    return jax.shard_map(
        per_device,
        mesh=mesh,
        in_specs=(
            row, P("dp"), P(), P(), P(None, None, "mp"), P("mp"), P("mp"), P("mp", None), P(),
            P(), P(), P(None, "mp"), P("mp"), P("mp", None), P(), row,
        ),
        out_specs=(
            row, row, P(), P(), P(None, None, "mp"), P("mp"), P("mp"), P("mp", None), P(),
            P(), P(), P(None, "mp"), P("mp"), P("mp", None), P(),
        ),
        check_vma=False,
    )
```
